512 devices in a mesh: slab: 8 (over z_hi, y), brick: 64 (over z_lo, x, core).
Axes of the slice: x: 4, y: 4, z: 16 (z_hi: 2, z_lo: 8; z = z_hi * 8 + z_lo), core: 2. Of those that a mesh axis runs over, the one named last changes fastest.
Arguments:
- inputs: bfloat16 [256, 8, 128, 128], P('brick', None, 'slab'), may hold values from -6 to 6
- pre_first: bfloat16 [256, 8, 128, 128], P('brick', None, 'slab'), may hold values from -8 to 8
- occupancy: int32 [256, 8, 128], P('brick', None, 'slab'), may hold values 0 or 1
- grad_out: bfloat16 [256, 8, 128, 128], P('brick', None, 'slab'), may hold values from -6 to 6
- w_first: bfloat16 [27, 128, 128], replicated, may hold values from -0.109375 to 0.109375
- w_second: bfloat16 [27, 128, 128], replicated, may hold values from -0.109375 to 0.109375
Outputs:
- grad_in: bfloat16 [256, 8, 128, 128], P('brick', None, 'slab')
- grad_first: bfloat16 [27, 128, 128], replicated
- grad_second: bfloat16 [27, 128, 128], replicated
The draws below stay inside these ranges and needn't reach their ends.
All inputs are finite; a program needn't handle non-finite values. No bound on the sum of `occupancy` on one device may be relied on, other than what follows from the above.
Results may differ from the reference program's by a relative error of at most 0.0053.
Values may be sent and summed in bfloat16 or wider, within the bound.
A program may use at most 64 MiB of HBM per device.

```python
import jax
import jax.numpy as jnp

C = 128
NY = 8
NX = 256
NZ = 128
CELLS = 262144


def with_ends(entries, key, smallest, top_value):
    index_at = [jax.random.randint(jax.random.fold_in(key, axis), (), 0, length) for axis, length in enumerate(entries.shape)]
    widest = entries.shape.index(max(entries.shape))
    next_to = index_at[:widest] + [(index_at[widest] + 1) % entries.shape[widest]] + index_at[widest + 1:]
    return entries.at[tuple(index_at)].set(smallest).at[tuple(next_to)].set(top_value)


def shard_levels(rng, dims, split, least, high):
    def one(position, blocks):
        heights = jax.random.uniform(jax.random.fold_in(jax.random.fold_in(rng, 6), position), (blocks,), jnp.float32, least / len(split), high / len(split))
        return jnp.repeat(jnp.exp(heights), dims[position] // blocks).reshape((-1,) + (1,) * (len(dims) - position - 1))

    gain = one(*split[0])
    for cut in split[1:]:
        gain = gain * one(*cut)
    return gain


def normal_values(own_key, extent, scale, limit, split=(), held_as=jnp.bfloat16):
    array = jax.random.normal(own_key, extent, jnp.float32) * scale
    if len(split) > 0:
        array = shard_levels(own_key, extent, split, -0.22, 0.18) * array
    return jnp.clip(array, min=-limit, max=limit).astype(held_as)


def setup_inputs(seed: int = 0) -> dict:
    arg_keys = jax.random.split(jax.random.key(seed), 7)
    inputs = normal_values(arg_keys[0], (NX, NY, NZ, C), 1.0, 6.0, ((0, 64), (2, 8)))
    pre_first = normal_values(arg_keys[1], (NX, NY, NZ, C), 1.5, 8.0, ((0, 64), (2, 8)))
    occupancy = with_ends((jax.random.randint(arg_keys[2], (NX, NY, NZ), 0, 10) < 1).astype(jnp.int32), jax.random.fold_in(arg_keys[2], 1), 0, 1)
    grad_out = normal_values(arg_keys[3], (NX, NY, NZ, C), 1.0, 6.0, ((0, 64), (2, 8)))
    w_first = normal_values(arg_keys[4], (27, C, C), (27 * C) ** -0.5, 0.109375)
    w_second = normal_values(arg_keys[5], (27, C, C), (27 * C) ** -0.5, 0.109375)
    return dict(inputs=inputs, pre_first=pre_first, occupancy=occupancy, grad_out=grad_out, w_first=w_first, w_second=w_second)


def offsets():
    return [(a, b, c) for a in (-1, 0, 1) for b in (-1, 0, 1) for c in (-1, 0, 1)]

def transpose_conv(field, kernel):
    chans = field.shape[-1]
    total = jnp.zeros((field.shape[0] * field.shape[1] * field.shape[2], chans), jnp.float32)
    for index, (a, b, c) in enumerate(offsets()):
        rolled = jnp.roll(field, shift=(a, b, c), axis=(0, 1, 2)).reshape(-1, chans)
        total = total + jnp.dot(rolled, kernel[index].T, preferred_element_type=jnp.float32)
    return total.reshape(field.shape)

def kernel_grad(left, field):
    chans = field.shape[-1]
    flat_left = left.reshape(-1, chans)
    parts = []
    for a, b, c in offsets():
        rolled = jnp.roll(field, shift=(a, b, c), axis=(0, 1, 2)).reshape(-1, chans)
        parts.append(jnp.dot(flat_left.T, rolled, preferred_element_type=jnp.float32))
    return jnp.stack(parts, axis=0)

def reference(inputs, pre_first, occupancy, grad_out, w_first, w_second):
    scale = 10.0 / jnp.sqrt(jnp.float32(CELLS))
    occ = occupancy.astype(jnp.float32)[..., None]
    pre = pre_first.astype(jnp.float32)
    sig = jax.nn.sigmoid(pre)
    act = (pre * sig * occ).astype(jnp.bfloat16)
    grad_second_pre = (grad_out.astype(jnp.float32) * occ).astype(jnp.bfloat16)
    grad_act = transpose_conv(grad_second_pre, w_second)
    grad_second = (kernel_grad(act, grad_second_pre) * scale).astype(jnp.bfloat16)
    grad_first_pre = (grad_act * occ * sig * (1.0 + pre * (1.0 - sig))).astype(jnp.bfloat16)
    grad_in = (grad_out.astype(jnp.float32) + transpose_conv(grad_first_pre, w_first)).astype(jnp.bfloat16)
    grad_first = (kernel_grad(inputs, grad_first_pre) * scale).astype(jnp.bfloat16)
    return (grad_in, grad_first, grad_second)
```

```python
import jax
import jax.numpy as jnp
from jax import lax
from jax.experimental import pallas as pl
from jax.experimental.pallas import tpu as pltpu
from jax.sharding import PartitionSpec as P


def with_halo(shard, sides, width):
    for axis, dim in sides:
        size, length = (lax.axis_size(axis), shard.shape[dim])
        up = [(i, (i + 1) % size) for i in range(size)]
        down = [(j, i) for i, j in up]
        last = lax.slice_in_dim(shard, length - width, length, axis=dim)
        initial = lax.slice_in_dim(shard, 0, width, axis=dim)
        before = lax.ppermute(last, axis, up)
        after = lax.ppermute(initial, axis, down)
        shard = jnp.concatenate([before, shard, after], axis=dim)
    return shard


def extend(field):
    padded = with_halo(field, (("slab", 2), ("brick", 0)), 1)
    return jnp.concatenate([padded[:, -1:], padded, padded[:, :1]], axis=1)


def columns(field):
    size_x, size_y, size_z, chans = field.shape
    padded = extend(field)
    pieces = []
    for a in (-1, 0, 1):
        for b in (-1, 0, 1):
            for c in (-1, 0, 1):
                pieces.append(
                    padded[1 - a : 1 - a + size_x, 1 - b : 1 - b + size_y, 1 - c : 1 - c + size_z]
                )
    stacked = jnp.concatenate(pieces, axis=-1)
    return stacked.reshape(size_x * size_y * size_z, 27 * chans)


def stacked_kernel(kernel):
    chans = kernel.shape[1]
    return jnp.transpose(kernel, (0, 2, 1)).reshape(27 * chans, chans)


def local_term(left, cols):
    chans = left.shape[-1]
    flat_left = left.reshape(-1, chans)
    term = lax.dot_general(
        flat_left, cols, (((0,), (0,)), ((), ())), preferred_element_type=jnp.float32
    )
    return term.reshape(chans, 27, chans).transpose(1, 0, 2)


ROWS, PADDED, PIECE, TILE, SIDE, DEPTH = 432, 448, 112, 16, 4, 16


def coordinates():
    slab, brick = lax.axis_index("slab"), lax.axis_index("brick")
    return (brick // 2) % 4, slab % 4, (slab // 4) * 8 + brick // 8, brick % 2


def device(x, y, z, core):
    return ((z // 8) * 4 + y, (z % 8) * 8 + x * 2 + core)


def reduce_body(scale, part, out, pair, summed, first_in, second_out, second_in, tiles, deep_in, final, sems):
    x, y, z, core = coordinates()
    pair_s, pair_r, first_s, first_r, second_s, second_r, deep_s, deep_r, back_s, back_r = sems[:10]
    up2_s, up2_r, up1_s, up1_r, last_s, last_r = sems[10:]
    partner = device(x, y, z, 1 - core)
    own = (x, y)

    def peer(axis, d):
        if axis == 0:
            return device((x + d) % SIDE, y, z, core)
        return device(x, (y + d) % SIDE, z, core)

    def deep(d):
        return device(x, y, (z + d) % DEPTH, core)

    def send(src, dst, s, r, to):
        return pltpu.make_async_remote_copy(
            src_ref=src, dst_ref=dst, send_sem=s, recv_sem=r, device_id=to,
            device_id_type=pl.DeviceIdType.MESH,
        )

    barrier = pltpu.get_barrier_semaphore()
    everyone = [partner] + [peer(h, d) for h in (0, 1) for d in (1, 2, 3)] + [deep(d) for d in range(1, DEPTH)]
    for to in everyone:
        pl.semaphore_signal(barrier, inc=1, device_id=to, device_id_type=pl.DeviceIdType.MESH)
    pl.semaphore_wait(barrier, len(everyone))

    order = (2, 1, 3, 0)
    pairs = {}
    for d in order:
        for h in (0, 1):
            slot = (own[h] + d) % SIDE
            pairs[h, d] = send(part.at[1 - core, h, slot], pair.at[h, slot], pair_s.at[h, d], pair_r.at[h, d], partner)
            pairs[h, d].start()
    firsts = {}
    for d in order:
        for h in (0, 1):
            slot = (own[h] + d) % SIDE
            pairs[h, d].wait_recv()
            total = part[core, h, slot].astype(jnp.float32) + pair[h, slot].astype(jnp.float32)
            summed[h, slot] = total.astype(jnp.bfloat16)
            if d:
                firsts[h, d] = send(summed.at[h, slot], first_in.at[h, d - 1], first_s.at[h, d - 1], first_r.at[h, d - 1], peer(h, d))
                firsts[h, d].start()
    seconds = {}
    for h in (0, 1):
        for d in (1, 2, 3):
            firsts[h, d].wait_recv()
        total = summed[h, own[h]].astype(jnp.float32)
        for d in (1, 2, 3):
            total = total + first_in[h, d - 1].astype(jnp.float32)
        second_out[h] = total.astype(jnp.bfloat16).reshape(SIDE, PIECE, 128)
        for d in (2, 1, 3):
            slot = (own[1 - h] + d) % SIDE
            seconds[h, d] = send(second_out.at[h, slot], second_in.at[h, d - 1], second_s.at[h, d - 1], second_r.at[h, d - 1], peer(1 - h, d))
            seconds[h, d].start()
    tiles[14:16] = jnp.zeros((2, TILE, 128), jnp.bfloat16)
    for h in (0, 1):
        for d in (1, 2, 3):
            seconds[h, d].wait_recv()
        total = second_out[h, own[1 - h]].astype(jnp.float32)
        for d in (1, 2, 3):
            total = total + second_in[h, d - 1].astype(jnp.float32)
        tiles[7 * h : 7 * h + 7] = total.astype(jnp.bfloat16).reshape(7, TILE, 128)
    far = sorted(range(1, DEPTH), key=lambda d: -min(d, DEPTH - d))
    deeps = {}
    for d in far:
        deeps[d] = send(tiles.at[(z + d) % DEPTH], deep_in.at[d - 1], deep_s.at[d - 1], deep_r.at[d - 1], deep(d))
        deeps[d].start()
    total = tiles[z].astype(jnp.float32)
    for d in reversed(far):
        deeps[d].wait_recv()
        total = total + deep_in[d - 1].astype(jnp.float32)
    final[z] = (total * scale).astype(jnp.bfloat16)
    backs = {}
    for d in far:
        backs[d] = send(final.at[z], final.at[z], back_s.at[d - 1], back_r.at[d - 1], deep(d))
        backs[d].start()
    for d in reversed(far):
        backs[d].wait_recv()
    up2 = {}
    for h in (0, 1):
        rows = pl.ds(pl.multiple_of(own[1 - h] * PIECE, PIECE), PIECE)
        out[core, h, own[h], rows] = final[7 * h : 7 * h + 7].reshape(PIECE, 128)
        place = out.at[core, h, own[h], rows]
        for d in (2, 1, 3):
            up2[h, d] = send(place, place, up2_s.at[h, d - 1], up2_r.at[h, d - 1], peer(1 - h, d))
            up2[h, d].start()
    up1, lasts = {}, {}
    for h in (0, 1):
        for d in (1, 2, 3):
            up2[h, d].wait_recv()
        place = out.at[core, h, own[h]]
        for d in (2, 1, 3):
            up1[h, d] = send(place, place, up1_s.at[h, d - 1], up1_r.at[h, d - 1], peer(h, d))
            up1[h, d].start()
        lasts[h, 0] = send(place, place, last_s.at[h, 0], last_r.at[h, 0], partner)
        lasts[h, 0].start()
    for d in (1, 3, 2):
        for h in (0, 1):
            up1[h, d].wait_recv()
            place = out.at[core, h, (own[h] + SIDE - d) % SIDE]
            lasts[h, d] = send(place, place, last_s.at[h, d], last_r.at[h, d], partner)
            lasts[h, d].start()
    for group in (pairs, firsts, seconds, deeps, backs, up2, up1, lasts):
        for copy in group.values():
            copy.wait_send()
    for copy in lasts.values():
        copy.wait_recv()


def reduce_kernels(second_term, first_term, scale):
    part = jnp.stack([second_term, first_term]).astype(jnp.bfloat16).reshape(2, 2, SIDE, ROWS, 128)
    part = jnp.pad(part, ((0, 0), (0, 0), (0, 0), (0, PADDED - ROWS), (0, 0)))
    bf16 = jnp.bfloat16
    dma = pltpu.SemaphoreType.DMA
    shapes = [(2, 4), (2, 4), (2, 3), (2, 3), (2, 3), (2, 3), (15,), (15,), (15,), (15,), (2, 3), (2, 3), (2, 3), (2, 3), (2, 4), (2, 4)]

    def kernel(part, out, pair, summed, first_in, second_out, second_in, tiles, deep_in, final, *sems):
        reduce_body(scale, part, out, pair, summed, first_in, second_out, second_in, tiles, deep_in, final, sems)

    out = pl.pallas_call(
        kernel,
        out_shape=jax.ShapeDtypeStruct(part.shape, bf16),
        in_specs=[pl.BlockSpec(memory_space=pltpu.VMEM)],
        out_specs=pl.BlockSpec(memory_space=pltpu.VMEM),
        scratch_shapes=[
            pltpu.VMEM((2, SIDE, PADDED, 128), bf16),
            pltpu.VMEM((2, SIDE, PADDED, 128), bf16),
            pltpu.VMEM((2, 3, PADDED, 128), bf16),
            pltpu.VMEM((2, SIDE, PIECE, 128), bf16),
            pltpu.VMEM((2, 3, PIECE, 128), bf16),
            pltpu.VMEM((DEPTH, TILE, 128), bf16),
            pltpu.VMEM((DEPTH - 1, TILE, 128), bf16),
            pltpu.VMEM((DEPTH, TILE, 128), bf16),
        ] + [dma(s) for s in shapes],
        compiler_params=pltpu.CompilerParams(collective_id=0, has_side_effects=True),
        name="reduce_kernels",
    )(part)
    out = out[:, :, :, :ROWS].reshape(2, 27, 128, 128)
    return out[0], out[1]


def per_device(inputs, pre_first, occupancy, grad_out, w_first, w_second):
    size_x, size_y, size_z, chans = inputs.shape
    cells_all = size_x * lax.axis_size("brick") * size_y * size_z * lax.axis_size("slab")
    scale = 10.0 / cells_all**0.5
    occ = occupancy.astype(jnp.float32)[..., None]
    pre = pre_first.astype(jnp.float32)
    sig = jax.nn.sigmoid(pre)
    act = (pre * sig * occ).astype(jnp.bfloat16)
    grad_second_pre = (grad_out.astype(jnp.float32) * occ).astype(jnp.bfloat16)
    cols_second = columns(grad_second_pre)
    grad_act = jnp.dot(cols_second, stacked_kernel(w_second), preferred_element_type=jnp.float32)
    grad_act = grad_act.reshape(inputs.shape)
    second_term = local_term(act, cols_second)
    grad_first_pre = (grad_act * occ * sig * (1.0 + pre * (1.0 - sig))).astype(jnp.bfloat16)
    cols_first = columns(grad_first_pre)
    back = jnp.dot(cols_first, stacked_kernel(w_first), preferred_element_type=jnp.float32)
    grad_in = (grad_out.astype(jnp.float32) + back.reshape(inputs.shape)).astype(jnp.bfloat16)
    first_term = local_term(inputs, cols_first)
    grad_second, grad_first = reduce_kernels(second_term, first_term, scale)
    return (grad_in, grad_first, grad_second)


def solution(mesh):
    in_specs = (
        P("brick", None, "slab", None),
        P("brick", None, "slab", None),
        P("brick", None, "slab"),
        P("brick", None, "slab", None),
        P(),
        P(),
    )
    out_specs = (P("brick", None, "slab", None), P(), P())
    return jax.shard_map(
        per_device, mesh=mesh, in_specs=in_specs, out_specs=out_specs, check_vma=False
    )
```

```python
import jax
import jax.numpy as jnp
from jax import lax
from jax.experimental import pallas as pl
from jax.experimental.pallas import tpu as pltpu
from jax.sharding import PartitionSpec as P

ROWS, PADDED, PIECE, TILE, SIDE, DEPTH = 432, 448, 112, 16, 4, 16
F32, BF16 = jnp.float32, jnp.bfloat16
NEAR = [(0, 1), (0, -1), (1, 0), (-1, 0), (1, 1), (1, -1), (-1, 1), (-1, -1)]


def coordinates():
    slab, brick = lax.axis_index("slab"), lax.axis_index("brick")
    return (brick // 2) % 4, slab % 4, (slab // 4) * 8 + brick // 8, brick % 2


def device(x, y, z, core):
    return ((z // 8) * 4 + y, (z % 8) * 8 + x * 2 + core)


def neighbour(ds, db):
    slab, brick = lax.axis_index("slab"), lax.axis_index("brick")
    return ((slab + ds + 8) % 8, (brick + db + 64) % 64)


def send(src, dst, s, r, to):
    return pltpu.make_async_remote_copy(
        src_ref=src, dst_ref=dst, send_sem=s, recv_sem=r, device_id=to,
        device_id_type=pl.DeviceIdType.MESH,
    )


def exchange(own, base, face, zin, s, r):
    copies = []
    for n, (ds, db) in enumerate(NEAR):
        if ds == 0:
            src, dst = own(3 if db == 1 else 0), base.at[0 if db == 1 else 5]
        else:
            side = 0 if ds == 1 else 1
            if db == 0:
                src, dst = face.at[side], zin.at[side, pl.ds(1, 4)]
            else:
                src, dst = face.at[side, 3 if db == 1 else 0], zin.at[side, 0 if db == 1 else 5]
        copies.append(send(src, dst, s.at[n], r.at[n], neighbour(ds, db)))
    order = (2, 3, 4, 5, 6, 7, 0, 1)
    for n in order:
        copies[n].start()
    return copies


def shifted_copies(base, zin, ext):
    def step(i, carry):
        v = base[i]
        wide = v.astype(F32)
        row = lax.broadcasted_iota(jnp.int32, wide.shape, 1)
        before = jnp.broadcast_to(zin[0, i].astype(F32)[:, None, :], wide.shape)
        after = jnp.broadcast_to(zin[1, i].astype(F32)[:, None, :], wide.shape)
        low = jnp.where(row == 15, after, pltpu.roll(wide, 15, 1)).astype(BF16)
        high = jnp.where(row == 0, before, pltpu.roll(wide, 1, 1)).astype(BF16)
        for c, w in enumerate((low, v, high)):
            ext[c, i, pl.ds(1, 8)] = w
            ext[c, i, 0] = w[7]
            ext[c, i, 9] = w[0]
        return carry

    lax.fori_loop(0, 6, step, 0)


def triple(ext, a, b, order):
    parts = [ext[1 + c, pl.ds(1 - a, 4), pl.ds(1 - b, 8)].reshape(512, 128) for c in order]
    return jnp.concatenate(parts, axis=1)


def transpose_conv(ext, w):
    total = None
    for a in (-1, 0, 1):
        for b in (-1, 0, 1):
            k = 9 * (a + 1) + 3 * (b + 1)
            right = jnp.concatenate([w[k], w[k + 1], w[k + 2]], axis=1)
            term = lax.dot_general(triple(ext, a, b, (-1, 0, 1)), right, (((1,), (1,)), ((), ())), preferred_element_type=F32)
            total = term if total is None else total + term
    return total


def put(part, g, k, value):
    value = value.astype(BF16)
    for j in range(8):
        lo, hi = max(128 * k, ROWS * j), min(128 * k + 128, ROWS * j + ROWS)
        if lo < hi:
            part[g, j // 4, j % 4, lo - ROWS * j : hi - ROWS * j] = value[lo - 128 * k : hi - 128 * k]


def body(scale, inputs, gsp, act, slope, grad_out, faces, w1_hbm, w2_hbm, grad_in, out, w1, w2, bases, facebuf, zins, ext, part, pair, summed, first_in, second_out, second_in, tiles, deep_in, final, w_sem, halo_s, halo_r, sems):
    x, y, z, core = coordinates()
    pair_s, pair_r, first_s, first_r, second_s, second_r, deep_s, deep_r, back_s, back_r = sems[:10]
    up2_s, up2_r, up1_s, up1_r, last_s, last_r = sems[10:]
    partner = device(x, y, z, 1 - core)
    own = (x, y)

    def peer(axis, d):
        if axis == 0:
            return device((x + d) % SIDE, y, z, core)
        return device(x, (y + d) % SIDE, z, core)

    def deep(d):
        return device(x, y, (z + d) % DEPTH, core)

    barrier = pltpu.get_barrier_semaphore()
    everyone = [neighbour(ds, db) for ds, db in reversed(NEAR)] + [deep(d) for d in range(1, DEPTH)]
    everyone += [peer(h, d) for h in (0, 1) for d in (1, 2, 3)] + [partner]
    for to in everyone:
        pl.semaphore_signal(barrier, inc=1, device_id=to, device_id_type=pl.DeviceIdType.MESH)
    loads = [pltpu.make_async_copy(w2_hbm, w2, w_sem.at[0]), pltpu.make_async_copy(w1_hbm, w1, w_sem.at[1])]
    for load in loads:
        load.start()
    bases[0, pl.ds(1, 4)] = gsp[...]
    bases[1, pl.ds(1, 4)] = inputs[...]
    for g in (0, 1):
        for c in (0, 1):
            for i in range(SIDE):
                part[g, c, i, ROWS:] = jnp.zeros((PADDED - ROWS, 128), BF16)
    tiles[14:16] = jnp.zeros((2, TILE, 128), BF16)
    act_t = act[...].reshape(512, 128).T
    pl.semaphore_wait(barrier, len(everyone))

    halos = [None, None, None]
    for f, ref in ((0, gsp), (1, inputs)):
        halos[f] = exchange(lambda i, ref=ref: ref.at[i], bases.at[f], faces.at[f], zins.at[f], halo_s.at[f], halo_r.at[f])
    for copy in halos[0]:
        copy.wait_recv()
    shifted_copies(bases.at[0], zins.at[0], ext.at[0])

    pairs = {}
    order = (2, 1, 3, 0)

    def start_pairs(h):
        for d in order:
            slot = (own[h] + d) % SIDE
            pairs[h, d] = send(part.at[h, 1 - core, slot], pair.at[h, slot], pair_s.at[h, d], pair_r.at[h, d], partner)
            pairs[h, d].start()

    for a in (-1, 0, 1):
        for b in (-1, 0, 1):
            k = 9 * (a + 1) + 3 * (b + 1)
            term = jnp.dot(act_t, triple(ext.at[0], a, b, (-1, 0, 1)), preferred_element_type=F32)
            for c in range(3):
                put(part, 0, k + c, term[:, 128 * c : 128 * c + 128])
    start_pairs(0)
    loads[0].wait()
    grad_act = transpose_conv(ext.at[0], w2)
    grad_pre = (grad_act.reshape(4, 8, 16, 128) * slope[...]).astype(BF16)
    bases[2, pl.ds(1, 4)] = grad_pre
    wide = grad_pre.astype(F32)
    facebuf[0] = wide[:, :, 15, :].astype(BF16)
    facebuf[1] = wide[:, :, 0, :].astype(BF16)
    halos[2] = exchange(lambda i: bases.at[2, i + 1], bases.at[2], facebuf, zins.at[2], halo_s.at[2], halo_r.at[2])
    firsts = {}

    def start_firsts(h):
        for d in order:
            slot = (own[h] + d) % SIDE
            pairs[h, d].wait_recv()
            total = part[h, core, slot].astype(F32) + pair[h, slot].astype(F32)
            summed[h, slot] = total.astype(BF16)
            if d:
                firsts[h, d] = send(summed.at[h, slot], first_in.at[h, d - 1], first_s.at[h, d - 1], first_r.at[h, d - 1], peer(h, d))
                firsts[h, d].start()

    start_firsts(0)
    for copy in halos[1]:
        copy.wait_recv()
    shifted_copies(bases.at[1], zins.at[1], ext.at[1])
    grad_t = grad_pre.reshape(512, 128).T
    for a in (-1, 0, 1):
        for b in (-1, 0, 1):
            k = 9 * (a + 1) + 3 * (b + 1)
            term = jnp.dot(grad_t, triple(ext.at[1], -a, -b, (1, 0, -1)), preferred_element_type=F32)
            for c in range(3):
                put(part, 1, k + c, term[:, 128 * c : 128 * c + 128].T)
    start_pairs(1)
    start_firsts(1)
    seconds = {}
    for h in (0, 1):
        for d in (1, 2, 3):
            firsts[h, d].wait_recv()
        total = summed[h, own[h]].astype(F32)
        for d in (1, 2, 3):
            total = total + first_in[h, d - 1].astype(F32)
        second_out[h] = total.astype(BF16).reshape(SIDE, PIECE, 128)
        for d in (2, 1, 3):
            slot = (own[1 - h] + d) % SIDE
            seconds[h, d] = send(second_out.at[h, slot], second_in.at[h, d - 1], second_s.at[h, d - 1], second_r.at[h, d - 1], peer(1 - h, d))
            seconds[h, d].start()
    for h in (0, 1):
        for d in (1, 2, 3):
            seconds[h, d].wait_recv()
        total = second_out[h, own[1 - h]].astype(F32)
        for d in (1, 2, 3):
            total = total + second_in[h, d - 1].astype(F32)
        tiles[7 * h : 7 * h + 7] = total.astype(BF16).reshape(7, TILE, 128)
    far = sorted(range(1, DEPTH), key=lambda d: -min(d, DEPTH - d))
    deeps = {}
    for d in far:
        deeps[d] = send(tiles.at[(z + d) % DEPTH], deep_in.at[d - 1], deep_s.at[d - 1], deep_r.at[d - 1], deep(d))
        deeps[d].start()

    for copy in halos[2]:
        copy.wait_recv()
    shifted_copies(bases.at[2], zins.at[2], ext.at[0])
    loads[1].wait()
    back = transpose_conv(ext.at[0], w1)
    grad_in[...] = (grad_out[...].astype(F32) + back.reshape(4, 8, 16, 128)).astype(BF16)

    total = tiles[z].astype(F32)
    for d in reversed(far):
        deeps[d].wait_recv()
        total = total + deep_in[d - 1].astype(F32)
    final[z] = (total * scale).astype(BF16)
    backs = {}
    for d in far:
        backs[d] = send(final.at[z], final.at[z], back_s.at[d - 1], back_r.at[d - 1], deep(d))
        backs[d].start()
    for d in reversed(far):
        backs[d].wait_recv()
    up2 = {}
    for h in (0, 1):
        rows = pl.ds(pl.multiple_of(own[1 - h] * PIECE, PIECE), PIECE)
        out[h, core, own[h], rows] = final[7 * h : 7 * h + 7].reshape(PIECE, 128)
        place = out.at[h, core, own[h], rows]
        for d in (2, 1, 3):
            up2[h, d] = send(place, place, up2_s.at[h, d - 1], up2_r.at[h, d - 1], peer(1 - h, d))
            up2[h, d].start()
    up1, lasts = {}, {}
    for h in (0, 1):
        for d in (1, 2, 3):
            up2[h, d].wait_recv()
        place = out.at[h, core, own[h]]
        for d in (2, 1, 3):
            up1[h, d] = send(place, place, up1_s.at[h, d - 1], up1_r.at[h, d - 1], peer(h, d))
            up1[h, d].start()
        lasts[h, 0] = send(place, place, last_s.at[h, 0], last_r.at[h, 0], partner)
        lasts[h, 0].start()
    for d in (1, 3, 2):
        for h in (0, 1):
            up1[h, d].wait_recv()
            place = out.at[h, core, (own[h] + SIDE - d) % SIDE]
            lasts[h, d] = send(place, place, last_s.at[h, d], last_r.at[h, d], partner)
            lasts[h, d].start()
    for group in (pairs, firsts, seconds, deeps, backs, up2, up1, lasts):
        for copy in group.values():
            copy.wait_send()
    for copies in halos:
        for copy in copies:
            copy.wait_send()
    for copy in lasts.values():
        copy.wait_recv()


def per_device(inputs, pre_first, occupancy, grad_out, w_first, w_second):
    size_x, size_y, size_z, chans = inputs.shape
    cells_all = size_x * lax.axis_size("brick") * size_y * size_z * lax.axis_size("slab")
    scale = 10.0 / cells_all**0.5
    occ = occupancy.astype(F32)[..., None]
    pre = pre_first.astype(F32)
    sig = jax.nn.sigmoid(pre)
    act = (pre * sig * occ).astype(BF16)
    slope = occ * sig * (1.0 + pre * (1.0 - sig))
    gsp = (grad_out.astype(F32) * occ).astype(BF16)
    faces = jnp.stack([jnp.stack([f[:, :, 15], f[:, :, 0]]) for f in (gsp, inputs)])
    dma = pltpu.SemaphoreType.DMA
    shapes = [(2, 4), (2, 4), (2, 3), (2, 3), (2, 3), (2, 3), (15,), (15,), (15,), (15,), (2, 3), (2, 3), (2, 3), (2, 3), (2, 4), (2, 4)]

    def kernel(*refs):
        body(scale, *refs[:28], refs[28:])

    vmem = pl.BlockSpec(memory_space=pltpu.VMEM)
    hbm = pl.BlockSpec(memory_space=pl.ANY)
    grad_in, out = pl.pallas_call(
        kernel,
        out_shape=(
            jax.ShapeDtypeStruct(inputs.shape, BF16),
            jax.ShapeDtypeStruct((2, 2, SIDE, PADDED, 128), BF16),
        ),
        in_specs=[vmem] * 6 + [hbm] * 2,
        out_specs=(vmem, vmem),
        scratch_shapes=[
            pltpu.VMEM((27, 128, 128), BF16),
            pltpu.VMEM((27, 128, 128), BF16),
            pltpu.VMEM((3, 6, 8, 16, 128), BF16),
            pltpu.VMEM((2, 4, 8, 128), BF16),
            pltpu.VMEM((3, 2, 6, 8, 128), BF16),
            pltpu.VMEM((2, 3, 6, 10, 16, 128), BF16),
            pltpu.VMEM((2, 2, SIDE, PADDED, 128), BF16),
            pltpu.VMEM((2, SIDE, PADDED, 128), BF16),
            pltpu.VMEM((2, SIDE, PADDED, 128), BF16),
            pltpu.VMEM((2, 3, PADDED, 128), BF16),
            pltpu.VMEM((2, SIDE, PIECE, 128), BF16),
            pltpu.VMEM((2, 3, PIECE, 128), BF16),
            pltpu.VMEM((DEPTH, TILE, 128), BF16),
            pltpu.VMEM((DEPTH - 1, TILE, 128), BF16),
            pltpu.VMEM((DEPTH, TILE, 128), BF16),
            dma((2,)), dma((3, 8)), dma((3, 8)),
        ] + [dma(s) for s in shapes],
        compiler_params=pltpu.CompilerParams(collective_id=0, has_side_effects=True),
        name="block_backward",
    )(inputs, gsp, act, slope, grad_out, faces, w_first, w_second)
    out = out[:, :, :, :ROWS].reshape(2, 27, 128, 128)
    return (grad_in, out[1], out[0])


def solution(mesh):
    in_specs = (
        P("brick", None, "slab", None),
        P("brick", None, "slab", None),
        P("brick", None, "slab"),
        P("brick", None, "slab", None),
        P(),
        P(),
    )
    out_specs = (P("brick", None, "slab", None), P(), P())
    return jax.shard_map(
        per_device, mesh=mesh, in_specs=in_specs, out_specs=out_specs, check_vma=False
    )
```

```python
import jax
import jax.numpy as jnp
from jax import lax
from jax.experimental import pallas as pl
from jax.experimental.pallas import tpu as pltpu
from jax.sharding import PartitionSpec as P

ROWS, PADDED, HALF, PIECE, TILE, SIDE, DEPTH = 432, 448, 224, 112, 16, 4, 16
F32, BF16 = jnp.float32, jnp.bfloat16
NEAR = [(0, 1), (0, -1), (1, 0), (-1, 0), (1, 1), (1, -1), (-1, 1), (-1, -1)]


def coordinates():
    slab, brick = lax.axis_index("slab"), lax.axis_index("brick")
    return (brick // 2) % 4, slab % 4, (slab // 4) * 8 + brick // 8, brick % 2


def device(x, y, z, core):
    return ((z // 8) * 4 + y, (z % 8) * 8 + x * 2 + core)


def neighbour(ds, db):
    slab, brick = lax.axis_index("slab"), lax.axis_index("brick")
    return ((slab + ds + 8) % 8, (brick + db + 64) % 64)


def send(src, dst, s, r, to):
    return pltpu.make_async_remote_copy(
        src_ref=src, dst_ref=dst, send_sem=s, recv_sem=r, device_id=to,
        device_id_type=pl.DeviceIdType.MESH,
    )


def exchange(base, face, zin, s, r):
    copies = []
    for n, (ds, db) in enumerate(NEAR):
        if ds == 0:
            src, dst = base.at[4 if db == 1 else 1], base.at[0 if db == 1 else 5]
        else:
            side = 0 if ds == 1 else 1
            if db == 0:
                src, dst = face.at[side], zin.at[side, pl.ds(1, 4)]
            else:
                src, dst = face.at[side, 3 if db == 1 else 0], zin.at[side, 0 if db == 1 else 5]
        copies.append(send(src, dst, s.at[n], r.at[n], neighbour(ds, db)))
    order = (2, 3, 4, 5, 6, 7, 0, 1)
    for n in order:
        copies[n].start()
    return copies


def shifted_copies(base, zin, ext):
    def step(i, carry):
        v = base[i]
        wide = v.astype(F32)
        row = lax.broadcasted_iota(jnp.int32, wide.shape, 1)
        before = jnp.broadcast_to(zin[0, i].astype(F32)[:, None, :], wide.shape)
        after = jnp.broadcast_to(zin[1, i].astype(F32)[:, None, :], wide.shape)
        low = jnp.where(row == 15, after, pltpu.roll(wide, 15, 1)).astype(BF16)
        high = jnp.where(row == 0, before, pltpu.roll(wide, 1, 1)).astype(BF16)
        for c, w in enumerate((low, v, high)):
            ext[c, i, pl.ds(1, 8)] = w
            ext[c, i, 0] = w[7]
            ext[c, i, 9] = w[0]
        return carry

    lax.fori_loop(0, 6, step, 0)


def triple(ext, a, b, order):
    parts = [ext[1 + c, pl.ds(1 - a, 4), pl.ds(1 - b, 8)].reshape(512, 128) for c in order]
    return jnp.concatenate(parts, axis=1)


def transpose_conv(ext, w):
    total = None
    for a in (-1, 0, 1):
        for b in (-1, 0, 1):
            k = 9 * (a + 1) + 3 * (b + 1)
            right = jnp.concatenate([w[k], w[k + 1], w[k + 2]], axis=1)
            term = lax.dot_general(triple(ext, a, b, (-1, 0, 1)), right, (((1,), (1,)), ((), ())), preferred_element_type=F32)
            total = term if total is None else total + term
    return total


def put(part, g, k, value):
    value = value.astype(BF16)
    for j in range(8):
        lo, hi = max(128 * k, ROWS * j), min(128 * k + 128, ROWS * j + ROWS)
        if lo < hi:
            part[g, j % 2, j // 2, lo - ROWS * j : hi - ROWS * j] = value[lo - 128 * k : hi - 128 * k]


def body(scale, inputs_hbm, pre_hbm, occ_hbm, grad_out_hbm, w1_hbm, w2_hbm, grad_in, first_hbm, second_hbm, pre, occ_in, grad_out, act, slope, w1, w2, bases, faces, zins, ext, part, pair, summed, stage, mid, first_in, second_out, second_in, tiles, deep_in, final, out, load_sem, halo_s, halo_r, store_sem, sems):
    x, y, z, core = coordinates()
    pair_s, pair_r, first_s, first_r, second_s, second_r, deep_s, deep_r, back_s, back_r = sems[:10]
    up2_s, up2_r, up1_s, up1_r, last_s, last_r = sems[10:]
    partner = device(x, y, z, 1 - core)
    own = (x, y)

    def peer(axis, d):
        if axis == 0:
            return device((x + d) % SIDE, y, z, core)
        return device(x, (y + d) % SIDE, z, core)

    def deep(d):
        return device(x, y, (z + d) % DEPTH, core)

    barrier = pltpu.get_barrier_semaphore()
    everyone = [neighbour(ds, db) for ds, db in reversed(NEAR)] + [deep(d) for d in range(1, DEPTH)]
    everyone += [peer(h, d) for h in (0, 1) for d in (1, 2, 3)] + [partner]
    for to in everyone:
        pl.semaphore_signal(barrier, inc=1, device_id=to, device_id_type=pl.DeviceIdType.MESH)
    loads = [
        pltpu.make_async_copy(src, dst, load_sem.at[n])
        for n, (src, dst) in enumerate(
            (
                (occ_hbm, occ_in),
                (grad_out_hbm, grad_out),
                (inputs_hbm, bases.at[1, pl.ds(1, 4)]),
                (pre_hbm, pre),
                (w2_hbm, w2),
                (w1_hbm, w1),
            )
        )
    ]
    for load in loads:
        load.start()
    for g in (0, 1):
        for c in (0, 1):
            for i in range(SIDE):
                part[g, c, i, ROWS:] = jnp.zeros((PADDED - ROWS, 128), BF16)
    tiles[14:16] = jnp.zeros((2, TILE, 128), BF16)

    def mask(i):
        row = occ_in[i].astype(F32)
        wide = jnp.broadcast_to(row[:, None, :], (8, 16, 16))
        here = lax.broadcasted_iota(jnp.int32, wide.shape, 1) == lax.broadcasted_iota(jnp.int32, wide.shape, 2)
        return jnp.sum(jnp.where(here, wide, 0.0), axis=2, keepdims=True)

    def set_faces(f, i, value):
        faces[f, 0, i] = value[:, 15, :].astype(BF16)
        faces[f, 1, i] = value[:, 0, :].astype(BF16)

    def masked(i, carry):
        value = grad_out[i].astype(F32) * mask(i)
        bases[0, i + 1] = value.astype(BF16)
        set_faces(0, i, value)
        set_faces(1, i, bases[1, i + 1].astype(F32))
        return carry

    for n in (0, 1, 2):
        loads[n].wait()
    lax.fori_loop(0, 4, masked, 0)
    pl.semaphore_wait(barrier, len(everyone))

    halos = [exchange(bases.at[f], faces.at[f], zins.at[f], halo_s.at[f], halo_r.at[f]) for f in (0, 1)]

    def pointwise(i, carry):
        v, occ = pre[i].astype(F32), mask(i)
        sig = 1.0 / (1.0 + jnp.exp(-v))
        act[i] = (v * sig * occ).astype(BF16)
        slope[i] = occ * sig * (1.0 + v * (1.0 - sig))
        return carry

    loads[3].wait()
    lax.fori_loop(0, 4, pointwise, 0)
    act_t = act[...].reshape(512, 128).T
    loads[4].wait()
    loads[5].wait()
    for copy in halos[0]:
        copy.wait_recv()
    shifted_copies(bases.at[0], zins.at[0], ext.at[0])

    pairs, firsts, seconds = {}, {}, {}

    def pair_copy(h, i):
        return send(part.at[h, 1 - core, i], pair.at[h, i], pair_s.at[h, i], pair_r.at[h, i], partner)

    def start_pairs(h, ab):
        for i in range(SIDE):
            if 384 * ab < 2 * ROWS * (i + 1) <= 384 * (ab + 1):
                pairs[h, i] = pair_copy(h, i)
                pairs[h, i].start()

    def start_firsts(h):
        def add(d):
            slot = (own[h] + d) % SIDE
            pair_copy(h, slot).wait_recv()
            total = part[h, core, slot].astype(F32) + pair[h, slot].astype(F32)
            summed[h, slot] = total.astype(BF16)
            return summed.at[h, slot]

        def go(n, src, dst, d):
            firsts[h, n] = send(src, dst, first_s.at[h, n], first_r.at[h, n], peer(h, d))
            firsts[h, n].start()

        low, high = pl.ds(0, HALF), pl.ds(HALF, HALF)
        ref = add(2)
        go(0, ref.at[low], stage.at[h, 0], 1)
        go(1, ref.at[high], stage.at[h, 1], 3)
        go(2, add(1).at[high], first_in.at[h, 0, high], 1)
        go(3, add(3).at[low], first_in.at[h, 1, low], 3)
        add(0)

    def forward_firsts(h):
        for n, d in ((0, 1), (1, 3)):
            slot = (own[h] + d) % SIDE
            rows = pl.ds(HALF * n, HALF)
            firsts[h, n].wait_recv()
            mid[h, n] = (summed[h, slot, rows].astype(F32) + stage[h, n].astype(F32)).astype(BF16)
            firsts[h, 4 + n] = send(mid.at[h, n], first_in.at[h, n, rows], first_s.at[h, 4 + n], first_r.at[h, 4 + n], peer(h, d))
            firsts[h, 4 + n].start()

    def start_seconds(h):
        for n in (2, 3, 4, 5):
            firsts[h, n].wait_recv()
        total = summed[h, own[h]].astype(F32) + first_in[h, 0].astype(F32) + first_in[h, 1].astype(F32)
        second_out[h] = total.astype(BF16).reshape(SIDE, PIECE, 128)
        for d in (2, 1, 3):
            slot = (own[1 - h] + d) % SIDE
            seconds[h, d] = send(second_out.at[h, slot], second_in.at[h, d - 1], second_s.at[h, d - 1], second_r.at[h, d - 1], peer(1 - h, d))
            seconds[h, d].start()

    for a in (-1, 0, 1):
        for b in (-1, 0, 1):
            k = 9 * (a + 1) + 3 * (b + 1)
            term = jnp.dot(act_t, triple(ext.at[0], a, b, (-1, 0, 1)), preferred_element_type=F32)
            for c in range(3):
                put(part, 0, k + c, term[:, 128 * c : 128 * c + 128])
            start_pairs(0, k // 3)
    grad_act = transpose_conv(ext.at[0], w2)
    grad_pre = (grad_act.reshape(4, 8, 16, 128) * slope[...]).astype(BF16)
    bases[2, pl.ds(1, 4)] = grad_pre
    wide = grad_pre.astype(F32)
    faces[2, 0] = wide[:, :, 15, :].astype(BF16)
    faces[2, 1] = wide[:, :, 0, :].astype(BF16)
    halos.append(exchange(bases.at[2], faces.at[2], zins.at[2], halo_s.at[2], halo_r.at[2]))
    start_firsts(0)
    for copy in halos[1]:
        copy.wait_recv()
    shifted_copies(bases.at[1], zins.at[1], ext.at[1])
    forward_firsts(0)
    grad_t = grad_pre.reshape(512, 128).T
    for a in (-1, 0, 1):
        for b in (-1, 0, 1):
            k = 9 * (a + 1) + 3 * (b + 1)
            term = jnp.dot(grad_t, triple(ext.at[1], -a, -b, (1, 0, -1)), preferred_element_type=F32)
            for c in range(3):
                put(part, 1, k + c, term[:, 128 * c : 128 * c + 128].T)
            start_pairs(1, k // 3)
    start_firsts(1)
    start_seconds(0)
    forward_firsts(1)
    start_seconds(1)
    for h in (0, 1):
        for d in (1, 2, 3):
            seconds[h, d].wait_recv()
        total = second_out[h, own[1 - h]].astype(F32)
        for d in (1, 2, 3):
            total = total + second_in[h, d - 1].astype(F32)
        tiles[7 * h : 7 * h + 7] = total.astype(BF16).reshape(7, TILE, 128)
    far = sorted(range(1, DEPTH), key=lambda d: -min(d, DEPTH - d))
    deeps = {}
    for d in far:
        deeps[d] = send(tiles.at[(z + d) % DEPTH], deep_in.at[d - 1], deep_s.at[d - 1], deep_r.at[d - 1], deep(d))
        deeps[d].start()

    for copy in halos[2]:
        copy.wait_recv()
    shifted_copies(bases.at[2], zins.at[2], ext.at[0])
    back = transpose_conv(ext.at[0], w1)
    grad_in[...] = (grad_out[...].astype(F32) + back.reshape(4, 8, 16, 128)).astype(BF16)

    total = tiles[z].astype(F32)
    for d in reversed(far):
        deeps[d].wait_recv()
        total = total + deep_in[d - 1].astype(F32)
    final[z] = (total * scale).astype(BF16)
    backs = {}
    for d in far:
        backs[d] = send(final.at[z], final.at[z], back_s.at[d - 1], back_r.at[d - 1], deep(d))
        backs[d].start()
    for d in reversed(far):
        backs[d].wait_recv()
    up2 = {}
    for h in (0, 1):
        rows = pl.ds(pl.multiple_of(own[1 - h] * PIECE, PIECE), PIECE)
        out[h, core, own[h], rows] = final[7 * h : 7 * h + 7].reshape(PIECE, 128)
        place = out.at[h, core, own[h], rows]
        for d in (2, 1, 3):
            up2[h, d] = send(place, place, up2_s.at[h, d - 1], up2_r.at[h, d - 1], peer(1 - h, d))
            up2[h, d].start()
    up1, lasts, stores = {}, {}, []

    def store(h, c, slot):
        rows = pl.ds(pl.multiple_of((2 * slot + c) * ROWS, TILE), ROWS)
        result = (second_hbm, first_hbm)[h]
        stores.append(pltpu.make_async_copy(out.at[h, c, slot, pl.ds(0, ROWS)], result.at[rows], store_sem.at[h, c, slot]))
        stores[-1].start()

    def up(h, n, place, d):
        up1[h, n] = send(place, place, up1_s.at[h, n], up1_r.at[h, n], peer(h, d))
        up1[h, n].start()

    def share(h, d):
        slot = (own[h] + d) % SIDE
        lasts[h, d] = send(out.at[h, core, slot], out.at[h, core, slot], last_s.at[h, d], last_r.at[h, d], partner)
        lasts[h, d].start()
        store(h, core, slot)

    for h in (0, 1):
        for d in (1, 2, 3):
            up2[h, d].wait_recv()
        up(h, 0, out.at[h, core, own[h]], 1)
        up(h, 1, out.at[h, core, own[h]], 3)
        share(h, 0)
    for n, came, d in ((0, 3, 1), (1, 1, 3)):
        for h in (0, 1):
            up1[h, n].wait_recv()
            up(h, 2 + n, out.at[h, core, (own[h] + came) % SIDE, pl.ds(HALF * n, HALF)], d)
            share(h, came)
    for d in (0, 3, 1):
        for h in (0, 1):
            lasts[h, d].wait_recv()
            store(h, 1 - core, (own[h] + d) % SIDE)
    for h in (0, 1):
        up1[h, 2].wait_recv()
        up1[h, 3].wait_recv()
        share(h, 2)
    for h in (0, 1):
        lasts[h, 2].wait_recv()
        store(h, 1 - core, (own[h] + 2) % SIDE)
    for group in (pairs, firsts, seconds, deeps, backs, up2, up1, lasts):
        for copy in group.values():
            copy.wait_send()
    for copies in halos:
        for copy in copies:
            copy.wait_send()
    for copy in stores:
        copy.wait()


def per_device(inputs, pre_first, occupancy, grad_out, w_first, w_second):
    size_x, size_y, size_z, chans = inputs.shape
    cells_all = size_x * lax.axis_size("brick") * size_y * size_z * lax.axis_size("slab")
    scale = 10.0 / cells_all**0.5
    dma = pltpu.SemaphoreType.DMA
    shapes = [(2, 4), (2, 4), (2, 6), (2, 6), (2, 3), (2, 3), (15,), (15,), (15,), (15,), (2, 3), (2, 3), (2, 4), (2, 4), (2, 4), (2, 4)]

    def kernel(*refs):
        body(scale, *refs[:36], refs[36:])

    vmem = pl.BlockSpec(memory_space=pltpu.VMEM)
    hbm = pl.BlockSpec(memory_space=pl.ANY)
    grad_in, grad_first, grad_second = pl.pallas_call(
        kernel,
        out_shape=(
            jax.ShapeDtypeStruct(inputs.shape, BF16),
            jax.ShapeDtypeStruct((8 * ROWS, 128), BF16),
            jax.ShapeDtypeStruct((8 * ROWS, 128), BF16),
        ),
        in_specs=[hbm] * 6,
        out_specs=(vmem, hbm, hbm),
        scratch_shapes=[
            pltpu.VMEM((4, 8, 16, 128), BF16),
            pltpu.VMEM((4, 8, 16), jnp.int32),
            pltpu.VMEM((4, 8, 16, 128), BF16),
            pltpu.VMEM((4, 8, 16, 128), BF16),
            pltpu.VMEM((4, 8, 16, 128), F32),
            pltpu.VMEM((27, 128, 128), BF16),
            pltpu.VMEM((27, 128, 128), BF16),
            pltpu.VMEM((3, 6, 8, 16, 128), BF16),
            pltpu.VMEM((3, 2, 4, 8, 128), BF16),
            pltpu.VMEM((3, 2, 6, 8, 128), BF16),
            pltpu.VMEM((2, 3, 6, 10, 16, 128), BF16),
            pltpu.VMEM((2, 2, SIDE, PADDED, 128), BF16),
            pltpu.VMEM((2, SIDE, PADDED, 128), BF16),
            pltpu.VMEM((2, SIDE, PADDED, 128), BF16),
            pltpu.VMEM((2, 2, HALF, 128), BF16),
            pltpu.VMEM((2, 2, HALF, 128), BF16),
            pltpu.VMEM((2, 2, PADDED, 128), BF16),
            pltpu.VMEM((2, SIDE, PIECE, 128), BF16),
            pltpu.VMEM((2, 3, PIECE, 128), BF16),
            pltpu.VMEM((DEPTH, TILE, 128), BF16),
            pltpu.VMEM((DEPTH - 1, TILE, 128), BF16),
            pltpu.VMEM((DEPTH, TILE, 128), BF16),
            pltpu.VMEM((2, 2, SIDE, PADDED, 128), BF16),
            dma((6,)), dma((3, 8)), dma((3, 8)), dma((2, 2, SIDE)),
        ] + [dma(s) for s in shapes],
        compiler_params=pltpu.CompilerParams(collective_id=0, has_side_effects=True),
        name="block_backward",
    )(inputs, pre_first, occupancy, grad_out, w_first, w_second)
    return (grad_in, grad_first.reshape(w_first.shape), grad_second.reshape(w_second.shape))


def solution(mesh):
    in_specs = (
        P("brick", None, "slab", None),
        P("brick", None, "slab", None),
        P("brick", None, "slab"),
        P("brick", None, "slab", None),
        P(),
        P(),
    )
    out_specs = (P("brick", None, "slab", None), P(), P())
    return jax.shard_map(
        per_device, mesh=mesh, in_specs=in_specs, out_specs=out_specs, check_vma=False
    )
```

```python
import jax
import jax.numpy as jnp
from jax import lax
from jax.experimental import pallas as pl
from jax.experimental.pallas import tpu as pltpu
from jax.sharding import PartitionSpec as P

ROWS, PADDED, HALF, PIECE, TILE, SIDE, DEPTH = 432, 448, 224, 112, 16, 4, 16
F32, BF16 = jnp.float32, jnp.bfloat16
NEAR = [(0, 1), (0, -1), (1, 0), (-1, 0), (1, 1), (1, -1), (-1, 1), (-1, -1)]


def coordinates():
    slab, brick = lax.axis_index("slab"), lax.axis_index("brick")
    return (brick // 2) % 4, slab % 4, (slab // 4) * 8 + brick // 8, brick % 2


def device(x, y, z, core):
    return ((z // 8) * 4 + y, (z % 8) * 8 + x * 2 + core)


def neighbour(ds, db):
    slab, brick = lax.axis_index("slab"), lax.axis_index("brick")
    return ((slab + ds + 8) % 8, (brick + db + 64) % 64)


def send(src, dst, s, r, to):
    return pltpu.make_async_remote_copy(
        src_ref=src, dst_ref=dst, send_sem=s, recv_sem=r, device_id=to,
        device_id_type=pl.DeviceIdType.MESH,
    )


def exchange(base, face, zin, s, r):
    copies = []
    for n, (ds, db) in enumerate(NEAR):
        if ds == 0:
            src, dst = base.at[4 if db == 1 else 1], base.at[0 if db == 1 else 5]
        else:
            side = 0 if ds == 1 else 1
            if db == 0:
                src, dst = face.at[side], zin.at[side, pl.ds(1, 4)]
            else:
                src, dst = face.at[side, 3 if db == 1 else 0], zin.at[side, 0 if db == 1 else 5]
        copies.append(send(src, dst, s.at[n], r.at[n], neighbour(ds, db)))
    order = (2, 3, 4, 5, 6, 7, 0, 1)
    for n in order:
        copies[n].start()
    return copies


def shifted_copies(base, zin, ext):
    def step(i, carry):
        v = base[i]
        wide = v.astype(F32)
        row = lax.broadcasted_iota(jnp.int32, wide.shape, 1)
        before = jnp.broadcast_to(zin[0, i].astype(F32)[:, None, :], wide.shape)
        after = jnp.broadcast_to(zin[1, i].astype(F32)[:, None, :], wide.shape)
        low = jnp.where(row == 15, after, pltpu.roll(wide, 15, 1)).astype(BF16)
        high = jnp.where(row == 0, before, pltpu.roll(wide, 1, 1)).astype(BF16)
        for c, w in enumerate((low, v, high)):
            ext[c, i, pl.ds(1, 8)] = w
            ext[c, i, 0] = w[7]
            ext[c, i, 9] = w[0]
        return carry

    lax.fori_loop(0, 6, step, 0)


def triple(ext, a, b, order):
    parts = [ext[1 + c, pl.ds(1 - a, 4), pl.ds(1 - b, 8)].reshape(512, 128) for c in order]
    return jnp.concatenate(parts, axis=1)


def transpose_conv(ext, w):
    total = None
    for a in (-1, 0, 1):
        for b in (-1, 0, 1):
            k = 9 * (a + 1) + 3 * (b + 1)
            right = jnp.concatenate([w[k], w[k + 1], w[k + 2]], axis=1)
            term = lax.dot_general(triple(ext, a, b, (-1, 0, 1)), right, (((1,), (1,)), ((), ())), preferred_element_type=F32)
            total = term if total is None else total + term
    return total


def put(part, g, k, value):
    value = value.astype(BF16)
    for j in range(8):
        lo, hi = max(128 * k, ROWS * j), min(128 * k + 128, ROWS * j + ROWS)
        if lo < hi:
            part[g, j % 2, j // 2, lo - ROWS * j : hi - ROWS * j] = value[lo - 128 * k : hi - 128 * k]


def body(scale, inputs_hbm, pre_hbm, occ_hbm, grad_out_hbm, w1_hbm, w2_hbm, grad_in, first_hbm, second_hbm, pre, occ_in, grad_out, act, slope, w1, w2, bases, faces, zins, ext, part, pair, summed, stage, mid, first_in, second_out, second_in, tiles, deep_in, final, out, load_sem, halo_s, halo_r, store_sem, sems):
    x, y, z, core = coordinates()
    pair_s, pair_r, first_s, first_r, second_s, second_r, deep_s, deep_r, back_s, back_r = sems[:10]
    up2_s, up2_r, up1_s, up1_r, last_s, last_r = sems[10:]
    partner = device(x, y, z, 1 - core)
    own = (x, y)

    def peer(axis, d):
        if axis == 0:
            return device((x + d) % SIDE, y, z, core)
        return device(x, (y + d) % SIDE, z, core)

    def deep(d):
        return device(x, y, (z + d) % DEPTH, core)

    barrier = pltpu.get_barrier_semaphore()
    everyone = [neighbour(ds, db) for ds, db in reversed(NEAR)] + [deep(d) for d in range(1, DEPTH)]
    everyone += [peer(h, d) for h in (0, 1) for d in (1, 2, 3)] + [partner]
    for to in everyone:
        pl.semaphore_signal(barrier, inc=1, device_id=to, device_id_type=pl.DeviceIdType.MESH)
    loads = [
        pltpu.make_async_copy(src, dst, load_sem.at[n])
        for n, (src, dst) in enumerate(
            (
                (occ_hbm, occ_in),
                (grad_out_hbm, grad_out),
                (inputs_hbm, bases.at[1, pl.ds(1, 4)]),
                (pre_hbm, pre),
                (w2_hbm, w2),
                (w1_hbm, w1),
            )
        )
    ]
    for load in loads:
        load.start()
    for g in (0, 1):
        for c in (0, 1):
            for i in range(SIDE):
                part[g, c, i, ROWS:] = jnp.zeros((PADDED - ROWS, 128), BF16)
    tiles[14:16] = jnp.zeros((2, TILE, 128), BF16)

    def mask(i):
        row = occ_in[i].astype(F32)
        wide = jnp.broadcast_to(row[:, None, :], (8, 16, 16))
        here = lax.broadcasted_iota(jnp.int32, wide.shape, 1) == lax.broadcasted_iota(jnp.int32, wide.shape, 2)
        return jnp.sum(jnp.where(here, wide, 0.0), axis=2, keepdims=True)

    def set_faces(f, i, value):
        faces[f, 0, i] = value[:, 15, :].astype(BF16)
        faces[f, 1, i] = value[:, 0, :].astype(BF16)

    def masked(i, carry):
        value = grad_out[i].astype(F32) * mask(i)
        bases[0, i + 1] = value.astype(BF16)
        set_faces(0, i, value)
        set_faces(1, i, bases[1, i + 1].astype(F32))
        return carry

    for n in (0, 1, 2):
        loads[n].wait()
    lax.fori_loop(0, 4, masked, 0)
    pl.semaphore_wait(barrier, len(everyone))

    halos = [exchange(bases.at[f], faces.at[f], zins.at[f], halo_s.at[f], halo_r.at[f]) for f in (0, 1)]

    def pointwise(i, carry):
        v, occ = pre[i].astype(F32), mask(i)
        sig = 1.0 / (1.0 + jnp.exp(-v))
        act[i] = (v * sig * occ).astype(BF16)
        slope[i] = occ * sig * (1.0 + v * (1.0 - sig))
        return carry

    loads[3].wait()
    lax.fori_loop(0, 4, pointwise, 0)
    act_t = act[...].reshape(512, 128).T
    loads[4].wait()
    loads[5].wait()
    for copy in halos[0]:
        copy.wait_recv()
    shifted_copies(bases.at[0], zins.at[0], ext.at[0])

    pairs, firsts, seconds = {}, {}, {}

    def pair_copy(h, i):
        return send(part.at[h, 1 - core, i], pair.at[h, i], pair_s.at[h, i], pair_r.at[h, i], partner)

    def start_pairs(h, ab):
        for i in range(SIDE):
            if 384 * ab < 2 * ROWS * (i + 1) <= 384 * (ab + 1):
                pairs[h, i] = pair_copy(h, i)
                pairs[h, i].start()

    def start_firsts(h):
        def add(d):
            slot = (own[h] + d) % SIDE
            pair_copy(h, slot).wait_recv()
            total = part[h, core, slot].astype(F32) + pair[h, slot].astype(F32)
            summed[h, slot] = total.astype(BF16)
            return summed.at[h, slot]

        def go(n, src, dst, d):
            firsts[h, n] = send(src, dst, first_s.at[h, n], first_r.at[h, n], peer(h, d))
            firsts[h, n].start()

        low, high = pl.ds(0, HALF), pl.ds(HALF, HALF)
        ref = add(2)
        go(0, ref.at[low], stage.at[h, 0], 1)
        go(1, ref.at[high], stage.at[h, 1], 3)
        go(2, add(1).at[high], first_in.at[h, 0, high], 1)
        go(3, add(3).at[low], first_in.at[h, 1, low], 3)
        add(0)

    def forward_firsts(h):
        for n, d in ((0, 1), (1, 3)):
            slot = (own[h] + d) % SIDE
            rows = pl.ds(HALF * n, HALF)
            firsts[h, n].wait_recv()
            mid[h, n] = (summed[h, slot, rows].astype(F32) + stage[h, n].astype(F32)).astype(BF16)
            firsts[h, 4 + n] = send(mid.at[h, n], first_in.at[h, n, rows], first_s.at[h, 4 + n], first_r.at[h, 4 + n], peer(h, d))
            firsts[h, 4 + n].start()

    def start_seconds(h):
        for n in (2, 3, 4, 5):
            firsts[h, n].wait_recv()
        total = summed[h, own[h]].astype(F32) + first_in[h, 0].astype(F32) + first_in[h, 1].astype(F32)
        second_out[h] = total.astype(BF16).reshape(SIDE, PIECE, 128)
        for d in (2, 1, 3):
            slot = (own[1 - h] + d) % SIDE
            seconds[h, d] = send(second_out.at[h, slot], second_in.at[h, d - 1], second_s.at[h, d - 1], second_r.at[h, d - 1], peer(1 - h, d))
            seconds[h, d].start()

    for a in (-1, 0, 1):
        for b in (-1, 0, 1):
            k = 9 * (a + 1) + 3 * (b + 1)
            term = jnp.dot(act_t, triple(ext.at[0], a, b, (-1, 0, 1)), preferred_element_type=F32)
            for c in range(3):
                put(part, 0, k + c, term[:, 128 * c : 128 * c + 128])
            start_pairs(0, k // 3)
    grad_act = transpose_conv(ext.at[0], w2)
    grad_pre = (grad_act.reshape(4, 8, 16, 128) * slope[...]).astype(BF16)
    bases[2, pl.ds(1, 4)] = grad_pre
    wide = grad_pre.astype(F32)
    faces[2, 0] = wide[:, :, 15, :].astype(BF16)
    faces[2, 1] = wide[:, :, 0, :].astype(BF16)
    halos.append(exchange(bases.at[2], faces.at[2], zins.at[2], halo_s.at[2], halo_r.at[2]))
    start_firsts(0)
    for copy in halos[1]:
        copy.wait_recv()
    shifted_copies(bases.at[1], zins.at[1], ext.at[1])
    forward_firsts(0)
    grad_t = grad_pre.reshape(512, 128).T
    for a in (-1, 0, 1):
        for b in (-1, 0, 1):
            k = 9 * (a + 1) + 3 * (b + 1)
            term = jnp.dot(grad_t, triple(ext.at[1], -a, -b, (1, 0, -1)), preferred_element_type=F32)
            for c in range(3):
                put(part, 1, k + c, term[:, 128 * c : 128 * c + 128].T)
            start_pairs(1, k // 3)
    start_firsts(1)
    start_seconds(0)
    forward_firsts(1)
    start_seconds(1)
    for h in (0, 1):
        for d in (1, 2, 3):
            seconds[h, d].wait_recv()
        total = second_out[h, own[1 - h]].astype(F32)
        for d in (1, 2, 3):
            total = total + second_in[h, d - 1].astype(F32)
        tiles[7 * h : 7 * h + 7] = total.astype(BF16).reshape(7, TILE, 128)
    far = sorted(range(1, DEPTH), key=lambda d: -min(d, DEPTH - d))
    deeps = {}
    for d in far:
        deeps[d] = send(tiles.at[(z + d) % DEPTH], deep_in.at[d - 1], deep_s.at[d - 1], deep_r.at[d - 1], deep(d))
        deeps[d].start()

    for copy in halos[2]:
        copy.wait_recv()
    shifted_copies(bases.at[2], zins.at[2], ext.at[0])
    back = transpose_conv(ext.at[0], w1)
    grad_in[...] = (grad_out[...].astype(F32) + back.reshape(4, 8, 16, 128)).astype(BF16)

    total = tiles[z].astype(F32)
    for d in reversed(far):
        deeps[d].wait_recv()
        total = total + deep_in[d - 1].astype(F32)
    final[z] = (total * scale).astype(BF16)
    backs = {}
    for d in far:
        backs[d] = send(final.at[z], final.at[z], back_s.at[d - 1], back_r.at[d - 1], deep(d))
        backs[d].start()
    for d in reversed(far):
        backs[d].wait_recv()
    up2 = {}
    for h in (0, 1):
        rows = pl.ds(pl.multiple_of(own[1 - h] * PIECE, PIECE), PIECE)
        out[h, core, own[h], rows] = final[7 * h : 7 * h + 7].reshape(PIECE, 128)
        place = out.at[h, core, own[h], rows]
        for d in (2, 1, 3):
            up2[h, d] = send(place, place, up2_s.at[h, d - 1], up2_r.at[h, d - 1], peer(1 - h, d))
            up2[h, d].start()
    up1, lasts, stores = {}, {}, []

    halves = (pl.ds(0, HALF), pl.ds(HALF, HALF))
    lengths = (HALF, ROWS - HALF)

    def store(h, c, slot, n):
        rows = pl.ds(pl.multiple_of((2 * slot + c) * ROWS + HALF * n, TILE), lengths[n])
        result = (second_hbm, first_hbm)[h]
        src = out.at[h, c, slot, pl.ds(HALF * n, lengths[n])]
        stores.append(pltpu.make_async_copy(src, result.at[rows], store_sem.at[h, c, slot, n]))
        stores[-1].start()

    def up(h, m, came, n, d):
        place = out.at[h, core, (own[h] + came) % SIDE, halves[n]]
        up1[h, m] = send(place, place, up1_s.at[h, m], up1_r.at[h, m], peer(h, d))
        up1[h, m].start()

    def share(h, came, n):
        slot = (own[h] + came) % SIDE
        place = out.at[h, core, slot, halves[n]]
        lasts[h, came, n] = send(place, place, last_s.at[h, came, n], last_r.at[h, came, n], partner)
        lasts[h, came, n].start()
        store(h, core, slot, n)

    def keep(h, came, n):
        lasts[h, came, n].wait_recv()
        store(h, 1 - core, (own[h] + came) % SIDE, n)

    for h in (0, 1):
        for d in (1, 2, 3):
            up2[h, d].wait_recv()
        up(h, 0, 0, 0, 1)
        up(h, 1, 0, 1, 3)
        up(h, 2, 0, 1, 1)
        up(h, 3, 0, 0, 3)
        share(h, 0, 0)
        share(h, 0, 1)
    for h in (0, 1):
        up1[h, 0].wait_recv()
        up(h, 4, 3, 0, 1)
        up1[h, 1].wait_recv()
        up(h, 5, 1, 1, 3)
        share(h, 3, 0)
        share(h, 1, 1)
    for h in (0, 1):
        up1[h, 2].wait_recv()
        share(h, 3, 1)
        up1[h, 3].wait_recv()
        share(h, 1, 0)
        for n in (0, 1):
            keep(h, 0, n)
        keep(h, 3, 0)
        keep(h, 1, 1)
    for h in (0, 1):
        up1[h, 4].wait_recv()
        share(h, 2, 0)
        up1[h, 5].wait_recv()
        share(h, 2, 1)
    for h in (0, 1):
        keep(h, 3, 1)
        keep(h, 1, 0)
    for h in (0, 1):
        for n in (0, 1):
            keep(h, 2, n)
    for group in (pairs, firsts, seconds, deeps, backs, up2, up1, lasts):
        for copy in group.values():
            copy.wait_send()
    for copies in halos:
        for copy in copies:
            copy.wait_send()
    for copy in stores:
        copy.wait()


def settle(sources, results, slots, sems):
    for n, (src, slot) in enumerate(zip(sources, slots)):
        pltpu.make_async_copy(src, slot, sems.at[0, n]).start()
    for n, (src, slot, dst) in enumerate(zip(sources, slots, results)):
        pltpu.make_async_copy(src, slot, sems.at[0, n]).wait()
        pltpu.make_async_copy(slot, dst, sems.at[1, n]).start()
    for n, (slot, dst) in enumerate(zip(slots, results)):
        pltpu.make_async_copy(slot, dst, sems.at[1, n]).wait()


def settled(*arrays):
    def kernel(*refs):
        count = len(arrays)
        sources, results, slots, sems = refs[:count], refs[count : 2 * count], refs[2 * count : 3 * count], refs[-1]
        cuts = [(n, pl.ds(i, a.shape[0] // parts)) for n, (a, parts) in enumerate(zip(arrays, (1, 3, 3)))
                for i in range(0, a.shape[0], a.shape[0] // parts)]
        settle(*([refs_[n].at[cut] for n, cut in cuts] for refs_ in (sources, results, slots)), sems)

    hbm = pl.BlockSpec(memory_space=pl.ANY)
    return pl.pallas_call(
        kernel,
        out_shape=tuple(jax.ShapeDtypeStruct(a.shape, a.dtype) for a in arrays),
        in_specs=[hbm] * len(arrays),
        out_specs=(hbm,) * len(arrays),
        scratch_shapes=[pltpu.VMEM(a.shape, a.dtype) for a in arrays] + [pltpu.SemaphoreType.DMA((2, 7))],
        name="settle",
    )(*arrays)


def per_device(inputs, pre_first, occupancy, grad_out, w_first, w_second):
    size_x, size_y, size_z, chans = inputs.shape
    cells_all = size_x * lax.axis_size("brick") * size_y * size_z * lax.axis_size("slab")
    scale = 10.0 / cells_all**0.5
    dma = pltpu.SemaphoreType.DMA
    shapes = [(2, 4), (2, 4), (2, 6), (2, 6), (2, 3), (2, 3), (15,), (15,), (15,), (15,), (2, 3), (2, 3), (2, 6), (2, 6), (2, 4, 2), (2, 4, 2)]

    def kernel(*refs):
        body(scale, *refs[:36], refs[36:])

    vmem = pl.BlockSpec(memory_space=pltpu.VMEM)
    hbm = pl.BlockSpec(memory_space=pl.ANY)
    grad_in, grad_first, grad_second = pl.pallas_call(
        kernel,
        out_shape=(
            jax.ShapeDtypeStruct(inputs.shape, BF16),
            jax.ShapeDtypeStruct((8 * ROWS, 128), BF16),
            jax.ShapeDtypeStruct((8 * ROWS, 128), BF16),
        ),
        in_specs=[hbm] * 6,
        out_specs=(vmem, hbm, hbm),
        scratch_shapes=[
            pltpu.VMEM((4, 8, 16, 128), BF16),
            pltpu.VMEM((4, 8, 16), jnp.int32),
            pltpu.VMEM((4, 8, 16, 128), BF16),
            pltpu.VMEM((4, 8, 16, 128), BF16),
            pltpu.VMEM((4, 8, 16, 128), F32),
            pltpu.VMEM((27, 128, 128), BF16),
            pltpu.VMEM((27, 128, 128), BF16),
            pltpu.VMEM((3, 6, 8, 16, 128), BF16),
            pltpu.VMEM((3, 2, 4, 8, 128), BF16),
            pltpu.VMEM((3, 2, 6, 8, 128), BF16),
            pltpu.VMEM((2, 3, 6, 10, 16, 128), BF16),
            pltpu.VMEM((2, 2, SIDE, PADDED, 128), BF16),
            pltpu.VMEM((2, SIDE, PADDED, 128), BF16),
            pltpu.VMEM((2, SIDE, PADDED, 128), BF16),
            pltpu.VMEM((2, 2, HALF, 128), BF16),
            pltpu.VMEM((2, 2, HALF, 128), BF16),
            pltpu.VMEM((2, 2, PADDED, 128), BF16),
            pltpu.VMEM((2, SIDE, PIECE, 128), BF16),
            pltpu.VMEM((2, 3, PIECE, 128), BF16),
            pltpu.VMEM((DEPTH, TILE, 128), BF16),
            pltpu.VMEM((DEPTH - 1, TILE, 128), BF16),
            pltpu.VMEM((DEPTH, TILE, 128), BF16),
            pltpu.VMEM((2, 2, SIDE, PADDED, 128), BF16),
            dma((6,)), dma((3, 8)), dma((3, 8)), dma((2, 2, SIDE, 2)),
        ] + [dma(s) for s in shapes],
        compiler_params=pltpu.CompilerParams(collective_id=0, has_side_effects=True),
        name="block_backward",
    )(inputs, pre_first, occupancy, grad_out, w_first, w_second)
    return settled(grad_in, grad_first.reshape(w_first.shape), grad_second.reshape(w_second.shape))


def solution(mesh):
    in_specs = (
        P("brick", None, "slab", None),
        P("brick", None, "slab", None),
        P("brick", None, "slab"),
        P("brick", None, "slab", None),
        P(),
        P(),
    )
    out_specs = (P("brick", None, "slab", None), P(), P())
    return jax.shard_map(
        per_device, mesh=mesh, in_specs=in_specs, out_specs=out_specs, check_vma=False
    )
```

```python
import jax
import jax.numpy as jnp
from jax import lax
from jax.experimental import pallas as pl
from jax.experimental.pallas import tpu as pltpu
from jax.sharding import PartitionSpec as P

ROWS, PADDED, HALF, PIECE, TILE, SIDE, DEPTH = 432, 448, 224, 112, 16, 4, 16
F32, BF16 = jnp.float32, jnp.bfloat16
NEAR = [(0, 1), (0, -1), (1, 0), (-1, 0), (1, 1), (1, -1), (-1, 1), (-1, -1)]


def coordinates():
    slab, brick = lax.axis_index("slab"), lax.axis_index("brick")
    return (brick // 2) % 4, slab % 4, (slab // 4) * 8 + brick // 8, brick % 2


def device(x, y, z, core):
    return ((z // 8) * 4 + y, (z % 8) * 8 + x * 2 + core)


def neighbour(ds, db):
    slab, brick = lax.axis_index("slab"), lax.axis_index("brick")
    return ((slab + ds + 8) % 8, (brick + db + 64) % 64)


def send(src, dst, s, r, to):
    return pltpu.make_async_remote_copy(
        src_ref=src, dst_ref=dst, send_sem=s, recv_sem=r, device_id=to,
        device_id_type=pl.DeviceIdType.MESH,
    )


def exchange(base, face, zin, s, r):
    copies = []
    for n, (ds, db) in enumerate(NEAR):
        if ds == 0:
            src, dst = base.at[4 if db == 1 else 1], base.at[0 if db == 1 else 5]
        else:
            side = 0 if ds == 1 else 1
            if db == 0:
                src, dst = face.at[side], zin.at[side, pl.ds(1, 4)]
            else:
                src, dst = face.at[side, 3 if db == 1 else 0], zin.at[side, 0 if db == 1 else 5]
        copies.append(send(src, dst, s.at[n], r.at[n], neighbour(ds, db)))
    order = (2, 3, 4, 5, 6, 7, 0, 1)
    for n in order:
        copies[n].start()
    return copies


def shifted_copies(base, zin, ext):
    def step(i, carry):
        v = base[i]
        wide = v.astype(F32)
        row = lax.broadcasted_iota(jnp.int32, wide.shape, 1)
        before = jnp.broadcast_to(zin[0, i].astype(F32)[:, None, :], wide.shape)
        after = jnp.broadcast_to(zin[1, i].astype(F32)[:, None, :], wide.shape)
        low = jnp.where(row == 15, after, pltpu.roll(wide, 15, 1)).astype(BF16)
        high = jnp.where(row == 0, before, pltpu.roll(wide, 1, 1)).astype(BF16)
        for c, w in enumerate((low, v, high)):
            ext[c, i, pl.ds(1, 8)] = w
            ext[c, i, 0] = w[7]
            ext[c, i, 9] = w[0]
        return carry

    lax.fori_loop(0, 6, step, 0)


def triple(ext, a, b, order):
    parts = [ext[1 + c, pl.ds(1 - a, 4), pl.ds(1 - b, 8)].reshape(512, 128) for c in order]
    return jnp.concatenate(parts, axis=1)


def transpose_conv(ext, w):
    total = None
    for a in (-1, 0, 1):
        for b in (-1, 0, 1):
            k = 9 * (a + 1) + 3 * (b + 1)
            right = jnp.concatenate([w[k], w[k + 1], w[k + 2]], axis=1)
            term = lax.dot_general(triple(ext, a, b, (-1, 0, 1)), right, (((1,), (1,)), ((), ())), preferred_element_type=F32)
            total = term if total is None else total + term
    return total


def put(part, g, k, value):
    value = value.astype(BF16)
    for j in range(8):
        lo, hi = max(128 * k, ROWS * j), min(128 * k + 128, ROWS * j + ROWS)
        if lo < hi:
            part[g, j % 2, j // 2, lo - ROWS * j : hi - ROWS * j] = value[lo - 128 * k : hi - 128 * k]


def body(scale, inputs_hbm, pre_hbm, occ_hbm, grad_out_hbm, w1_hbm, w2_hbm, grad_in, first_hbm, second_hbm, pre, occ_in, grad_out, act, slope, w1, w2, bases, faces, zins, ext, part, pair, summed, stage, mid, first_in, second_out, second_in, tiles, deep_in, final, out, load_sem, halo_s, halo_r, store_sem, sems):
    x, y, z, core = coordinates()
    pair_s, pair_r, first_s, first_r, second_s, second_r, deep_s, deep_r, back_s, back_r = sems[:10]
    up2_s, up2_r, up1_s, up1_r, last_s, last_r = sems[10:]
    partner = device(x, y, z, 1 - core)
    own = (x, y)

    def peer(axis, d):
        if axis == 0:
            return device((x + d) % SIDE, y, z, core)
        return device(x, (y + d) % SIDE, z, core)

    def deep(d):
        return device(x, y, (z + d) % DEPTH, core)

    barrier = pltpu.get_barrier_semaphore()
    everyone = [neighbour(ds, db) for ds, db in reversed(NEAR)] + [deep(d) for d in range(1, DEPTH)]
    everyone += [peer(h, d) for h in (0, 1) for d in (1, 2, 3)] + [partner]
    for to in everyone:
        pl.semaphore_signal(barrier, inc=1, device_id=to, device_id_type=pl.DeviceIdType.MESH)
    loads = [
        pltpu.make_async_copy(src, dst, load_sem.at[n])
        for n, (src, dst) in enumerate(
            (
                (occ_hbm, occ_in),
                (grad_out_hbm, grad_out),
                (inputs_hbm, bases.at[1, pl.ds(1, 4)]),
                (pre_hbm, pre),
                (w2_hbm, w2),
                (w1_hbm, w1),
            )
        )
    ]
    for load in loads:
        load.start()
    for g in (0, 1):
        for c in (0, 1):
            for i in range(SIDE):
                part[g, c, i, ROWS:] = jnp.zeros((PADDED - ROWS, 128), BF16)

    def mask(i):
        row = occ_in[i].astype(F32)
        wide = jnp.broadcast_to(row[:, None, :], (8, 16, 16))
        here = lax.broadcasted_iota(jnp.int32, wide.shape, 1) == lax.broadcasted_iota(jnp.int32, wide.shape, 2)
        return jnp.sum(jnp.where(here, wide, 0.0), axis=2, keepdims=True)

    def set_faces(f, i, value):
        faces[f, 0, i] = value[:, 15, :].astype(BF16)
        faces[f, 1, i] = value[:, 0, :].astype(BF16)

    def masked(i, carry):
        value = grad_out[i].astype(F32) * mask(i)
        bases[0, i + 1] = value.astype(BF16)
        set_faces(0, i, value)
        set_faces(1, i, bases[1, i + 1].astype(F32))
        return carry

    for n in (0, 1, 2):
        loads[n].wait()
    lax.fori_loop(0, 4, masked, 0)
    pl.semaphore_wait(barrier, len(everyone))

    halos = [exchange(bases.at[f], faces.at[f], zins.at[f], halo_s.at[f], halo_r.at[f]) for f in (0, 1)]

    def pointwise(i, carry):
        v, occ = pre[i].astype(F32), mask(i)
        sig = 1.0 / (1.0 + jnp.exp(-v))
        act[i] = (v * sig * occ).astype(BF16)
        slope[i] = occ * sig * (1.0 + v * (1.0 - sig))
        return carry

    loads[3].wait()
    lax.fori_loop(0, 4, pointwise, 0)
    act_t = act[...].reshape(512, 128).T
    loads[4].wait()
    loads[5].wait()
    for copy in halos[0]:
        copy.wait_recv()
    shifted_copies(bases.at[0], zins.at[0], ext.at[0])

    pairs, firsts, seconds = {}, {}, {}

    def pair_copy(h, i):
        return send(part.at[h, 1 - core, i], pair.at[h, i], pair_s.at[h, i], pair_r.at[h, i], partner)

    def start_pairs(h, ab):
        for i in range(SIDE):
            if 384 * ab < 2 * ROWS * (i + 1) <= 384 * (ab + 1):
                pairs[h, i] = pair_copy(h, i)
                pairs[h, i].start()

    def start_firsts(h):
        def add(d):
            slot = (own[h] + d) % SIDE
            pair_copy(h, slot).wait_recv()
            total = part[h, core, slot].astype(F32) + pair[h, slot].astype(F32)
            summed[h, slot] = total.astype(BF16)
            return summed.at[h, slot]

        def go(n, src, dst, d):
            firsts[h, n] = send(src, dst, first_s.at[h, n], first_r.at[h, n], peer(h, d))
            firsts[h, n].start()

        low, high = pl.ds(0, HALF), pl.ds(HALF, HALF)
        ref = add(2)
        go(0, ref.at[low], stage.at[h, 0], 1)
        go(1, ref.at[high], stage.at[h, 1], 3)
        go(2, add(1).at[high], first_in.at[h, 0, high], 1)
        go(3, add(3).at[low], first_in.at[h, 1, low], 3)
        add(0)

    def forward_firsts(h):
        for n, d in ((0, 1), (1, 3)):
            slot = (own[h] + d) % SIDE
            rows = pl.ds(HALF * n, HALF)
            firsts[h, n].wait_recv()
            mid[h, n] = (summed[h, slot, rows].astype(F32) + stage[h, n].astype(F32)).astype(BF16)
            firsts[h, 4 + n] = send(mid.at[h, n], first_in.at[h, n, rows], first_s.at[h, 4 + n], first_r.at[h, 4 + n], peer(h, d))
            firsts[h, 4 + n].start()

    def start_seconds(h):
        for n in (2, 3, 4, 5):
            firsts[h, n].wait_recv()
        total = summed[h, own[h]].astype(F32) + first_in[h, 0].astype(F32) + first_in[h, 1].astype(F32)
        second_out[h] = total.astype(BF16).reshape(SIDE, PIECE, 128)
        for d in (2, 1, 3):
            slot = (own[1 - h] + d) % SIDE
            seconds[h, d] = send(second_out.at[h, slot], second_in.at[h, d - 1], second_s.at[h, d - 1], second_r.at[h, d - 1], peer(1 - h, d))
            seconds[h, d].start()

    for a in (-1, 0, 1):
        for b in (-1, 0, 1):
            k = 9 * (a + 1) + 3 * (b + 1)
            term = jnp.dot(act_t, triple(ext.at[0], a, b, (-1, 0, 1)), preferred_element_type=F32)
            for c in range(3):
                put(part, 0, k + c, term[:, 128 * c : 128 * c + 128])
            start_pairs(0, k // 3)
    grad_act = transpose_conv(ext.at[0], w2)
    grad_pre = (grad_act.reshape(4, 8, 16, 128) * slope[...]).astype(BF16)
    bases[2, pl.ds(1, 4)] = grad_pre
    wide = grad_pre.astype(F32)
    faces[2, 0] = wide[:, :, 15, :].astype(BF16)
    faces[2, 1] = wide[:, :, 0, :].astype(BF16)
    halos.append(exchange(bases.at[2], faces.at[2], zins.at[2], halo_s.at[2], halo_r.at[2]))
    start_firsts(0)
    for copy in halos[1]:
        copy.wait_recv()
    shifted_copies(bases.at[1], zins.at[1], ext.at[1])
    forward_firsts(0)
    grad_t = grad_pre.reshape(512, 128).T
    for a in (-1, 0, 1):
        for b in (-1, 0, 1):
            k = 9 * (a + 1) + 3 * (b + 1)
            term = jnp.dot(grad_t, triple(ext.at[1], -a, -b, (1, 0, -1)), preferred_element_type=F32)
            for c in range(3):
                put(part, 1, k + c, term[:, 128 * c : 128 * c + 128].T)
            start_pairs(1, k // 3)
    far = sorted(range(1, DEPTH), key=lambda d: -min(d, DEPTH - d))
    owned = (range(0, 7), range(7, 14))

    def deep_copy(t):
        slot = (t - z + DEPTH) % DEPTH - 1
        return send(tiles.at[t], deep_in.at[slot], deep_s.at[t], deep_r.at[slot], device(x, y, t, core))

    def back_copy(d):
        return send(final.at[z], final.at[z], back_s.at[d], back_r.at[z], deep(d))

    def start_deeps(h):
        for d in (1, 2, 3):
            seconds[h, d].wait_recv()
        total = second_out[h, own[1 - h]].astype(F32)
        for d in (1, 2, 3):
            total = total + second_in[h, d - 1].astype(F32)
        tiles[7 * h : 7 * h + 7] = total.astype(BF16).reshape(7, TILE, 128)
        for t in owned[h]:

            @pl.when(z != t)
            def _():
                deep_copy(t).start()

    def start_backs(h):
        @pl.when(z // 7 == h)
        def _():
            total = tiles[z].astype(F32)
            for d in reversed(far):
                send(tiles.at[z], deep_in.at[d - 1], deep_s.at[0], deep_r.at[d - 1], deep(d)).wait_recv()
                total = total + deep_in[d - 1].astype(F32)
            final[z] = (total * scale).astype(BF16)
            for d in far:
                back_copy(d).start()

    def wait_backs(h):
        for t in owned[h]:

            @pl.when(z != t)
            def _():
                send(final.at[t], final.at[t], back_s.at[0], back_r.at[t], deep(1)).wait_recv()

    start_firsts(1)
    start_seconds(0)
    forward_firsts(1)
    start_deeps(0)
    start_seconds(1)
    start_deeps(1)
    start_backs(0)

    for copy in halos[2]:
        copy.wait_recv()
    shifted_copies(bases.at[2], zins.at[2], ext.at[0])
    back = transpose_conv(ext.at[0], w1)
    grad_in[...] = (grad_out[...].astype(F32) + back.reshape(4, 8, 16, 128)).astype(BF16)

    start_backs(1)
    up2 = {}
    for h in (0, 1):
        wait_backs(h)
        rows = pl.ds(pl.multiple_of(own[1 - h] * PIECE, PIECE), PIECE)
        out[h, core, own[h], rows] = final[7 * h : 7 * h + 7].reshape(PIECE, 128)
        place = out.at[h, core, own[h], rows]
        for d in (2, 1, 3):
            up2[h, d] = send(place, place, up2_s.at[h, d - 1], up2_r.at[h, d - 1], peer(1 - h, d))
            up2[h, d].start()
    up1, lasts, stores = {}, {}, []

    halves = (pl.ds(0, HALF), pl.ds(HALF, HALF))
    lengths = (HALF, ROWS - HALF)

    def store(h, c, slot, n):
        rows = pl.ds(pl.multiple_of((2 * slot + c) * ROWS + HALF * n, TILE), lengths[n])
        result = (second_hbm, first_hbm)[h]
        src = out.at[h, c, slot, pl.ds(HALF * n, lengths[n])]
        stores.append(pltpu.make_async_copy(src, result.at[rows], store_sem.at[h, c, slot, n]))
        stores[-1].start()

    def up(h, m, came, n, d):
        place = out.at[h, core, (own[h] + came) % SIDE, halves[n]]
        up1[h, m] = send(place, place, up1_s.at[h, m], up1_r.at[h, m], peer(h, d))
        up1[h, m].start()

    def share(h, came, n):
        slot = (own[h] + came) % SIDE
        place = out.at[h, core, slot, halves[n]]
        lasts[h, came, n] = send(place, place, last_s.at[h, came, n], last_r.at[h, came, n], partner)
        lasts[h, came, n].start()
        store(h, core, slot, n)

    def keep(h, came, n):
        lasts[h, came, n].wait_recv()
        store(h, 1 - core, (own[h] + came) % SIDE, n)

    def own_chunk(h):
        for d in (1, 2, 3):
            up2[h, d].wait_recv()
        up(h, 0, 0, 0, 1)
        up(h, 1, 0, 1, 3)
        up(h, 2, 0, 1, 1)
        up(h, 3, 0, 0, 3)
        share(h, 0, 0)
        share(h, 0, 1)

    def forward(h):
        up1[h, 0].wait_recv()
        up(h, 4, 3, 0, 1)
        up1[h, 1].wait_recv()
        up(h, 5, 1, 1, 3)
        share(h, 3, 0)
        share(h, 1, 1)

    def others(h):
        up1[h, 2].wait_recv()
        share(h, 3, 1)
        up1[h, 3].wait_recv()
        share(h, 1, 0)
        for n in (0, 1):
            keep(h, 0, n)
        keep(h, 3, 0)
        keep(h, 1, 1)

    def opposite(h):
        up1[h, 4].wait_recv()
        share(h, 2, 0)
        up1[h, 5].wait_recv()
        share(h, 2, 1)

    def rest(h):
        keep(h, 3, 1)
        keep(h, 1, 0)
        for n in (0, 1):
            keep(h, 2, n)

    own_chunk(0)
    forward(0)
    own_chunk(1)
    others(0)
    forward(1)
    opposite(0)
    others(1)
    opposite(1)
    rest(0)
    rest(1)
    for t in range(14):

        @pl.when(z != t)
        def _():
            deep_copy(t).wait_send()

    @pl.when(z < 14)
    def _():
        for d in range(1, DEPTH):
            back_copy(d).wait_send()

    for group in (pairs, firsts, seconds, up2, up1, lasts):
        for copy in group.values():
            copy.wait_send()
    for copies in halos:
        for copy in copies:
            copy.wait_send()
    for copy in stores:
        copy.wait()


def settle(sources, results, slots, sems):
    for n, (src, slot) in enumerate(zip(sources, slots)):
        pltpu.make_async_copy(src, slot, sems.at[0, n]).start()
    for n, (src, slot, dst) in enumerate(zip(sources, slots, results)):
        pltpu.make_async_copy(src, slot, sems.at[0, n]).wait()
        pltpu.make_async_copy(slot, dst, sems.at[1, n]).start()
    for n, (slot, dst) in enumerate(zip(slots, results)):
        pltpu.make_async_copy(slot, dst, sems.at[1, n]).wait()


def settled(*arrays):
    def kernel(*refs):
        count = len(arrays)
        sources, results, slots, sems = refs[:count], refs[count : 2 * count], refs[2 * count : 3 * count], refs[-1]
        cuts = [(n, pl.ds(i, a.shape[0] // parts)) for n, (a, parts) in enumerate(zip(arrays, (1, 3, 3)))
                for i in range(0, a.shape[0], a.shape[0] // parts)]
        settle(*([refs_[n].at[cut] for n, cut in cuts] for refs_ in (sources, results, slots)), sems)

    hbm = pl.BlockSpec(memory_space=pl.ANY)
    return pl.pallas_call(
        kernel,
        out_shape=tuple(jax.ShapeDtypeStruct(a.shape, a.dtype) for a in arrays),
        in_specs=[hbm] * len(arrays),
        out_specs=(hbm,) * len(arrays),
        scratch_shapes=[pltpu.VMEM(a.shape, a.dtype) for a in arrays] + [pltpu.SemaphoreType.DMA((2, 7))],
        name="settle",
    )(*arrays)


def per_device(inputs, pre_first, occupancy, grad_out, w_first, w_second):
    size_x, size_y, size_z, chans = inputs.shape
    cells_all = size_x * lax.axis_size("brick") * size_y * size_z * lax.axis_size("slab")
    scale = 10.0 / cells_all**0.5
    dma = pltpu.SemaphoreType.DMA
    shapes = [(2, 4), (2, 4), (2, 6), (2, 6), (2, 3), (2, 3), (16,), (16,), (16,), (16,), (2, 3), (2, 3), (2, 6), (2, 6), (2, 4, 2), (2, 4, 2)]

    def kernel(*refs):
        body(scale, *refs[:36], refs[36:])

    vmem = pl.BlockSpec(memory_space=pltpu.VMEM)
    hbm = pl.BlockSpec(memory_space=pl.ANY)
    grad_in, grad_first, grad_second = pl.pallas_call(
        kernel,
        out_shape=(
            jax.ShapeDtypeStruct(inputs.shape, BF16),
            jax.ShapeDtypeStruct((8 * ROWS, 128), BF16),
            jax.ShapeDtypeStruct((8 * ROWS, 128), BF16),
        ),
        in_specs=[hbm] * 6,
        out_specs=(vmem, hbm, hbm),
        scratch_shapes=[
            pltpu.VMEM((4, 8, 16, 128), BF16),
            pltpu.VMEM((4, 8, 16), jnp.int32),
            pltpu.VMEM((4, 8, 16, 128), BF16),
            pltpu.VMEM((4, 8, 16, 128), BF16),
            pltpu.VMEM((4, 8, 16, 128), F32),
            pltpu.VMEM((27, 128, 128), BF16),
            pltpu.VMEM((27, 128, 128), BF16),
            pltpu.VMEM((3, 6, 8, 16, 128), BF16),
            pltpu.VMEM((3, 2, 4, 8, 128), BF16),
            pltpu.VMEM((3, 2, 6, 8, 128), BF16),
            pltpu.VMEM((2, 3, 6, 10, 16, 128), BF16),
            pltpu.VMEM((2, 2, SIDE, PADDED, 128), BF16),
            pltpu.VMEM((2, SIDE, PADDED, 128), BF16),
            pltpu.VMEM((2, SIDE, PADDED, 128), BF16),
            pltpu.VMEM((2, 2, HALF, 128), BF16),
            pltpu.VMEM((2, 2, HALF, 128), BF16),
            pltpu.VMEM((2, 2, PADDED, 128), BF16),
            pltpu.VMEM((2, SIDE, PIECE, 128), BF16),
            pltpu.VMEM((2, 3, PIECE, 128), BF16),
            pltpu.VMEM((DEPTH, TILE, 128), BF16),
            pltpu.VMEM((DEPTH - 1, TILE, 128), BF16),
            pltpu.VMEM((DEPTH, TILE, 128), BF16),
            pltpu.VMEM((2, 2, SIDE, PADDED, 128), BF16),
            dma((6,)), dma((3, 8)), dma((3, 8)), dma((2, 2, SIDE, 2)),
        ] + [dma(s) for s in shapes],
        compiler_params=pltpu.CompilerParams(collective_id=0, has_side_effects=True),
        name="block_backward",
    )(inputs, pre_first, occupancy, grad_out, w_first, w_second)
    return settled(grad_in, grad_first.reshape(w_first.shape), grad_second.reshape(w_second.shape))


def solution(mesh):
    in_specs = (
        P("brick", None, "slab", None),
        P("brick", None, "slab", None),
        P("brick", None, "slab"),
        P("brick", None, "slab", None),
        P(),
        P(),
    )
    out_specs = (P("brick", None, "slab", None), P(), P())
    return jax.shard_map(
        per_device, mesh=mesh, in_specs=in_specs, out_specs=out_specs, check_vma=False
    )
```

```python
import jax
import jax.numpy as jnp
from jax import lax
from jax.experimental import pallas as pl
from jax.experimental.pallas import tpu as pltpu
from jax.sharding import PartitionSpec as P

ROWS, PADDED, HALF, PIECE, TILE, SIDE, DEPTH = 432, 448, 224, 112, 16, 4, 16
F32, BF16 = jnp.float32, jnp.bfloat16
NEAR = [(0, 1), (0, -1), (1, 0), (-1, 0), (1, 1), (1, -1), (-1, 1), (-1, -1)]


def coordinates():
    slab, brick = lax.axis_index("slab"), lax.axis_index("brick")
    return (brick // 2) % 4, slab % 4, (slab // 4) * 8 + brick // 8, brick % 2


def device(x, y, z, core):
    return ((z // 8) * 4 + y, (z % 8) * 8 + x * 2 + core)


def neighbour(ds, db):
    slab, brick = lax.axis_index("slab"), lax.axis_index("brick")
    return ((slab + ds + 8) % 8, (brick + db + 64) % 64)


def send(src, dst, s, r, to):
    return pltpu.make_async_remote_copy(
        src_ref=src, dst_ref=dst, send_sem=s, recv_sem=r, device_id=to,
        device_id_type=pl.DeviceIdType.MESH,
    )


def exchange(base, face, zin, s, r):
    copies = []
    for n, (ds, db) in enumerate(NEAR):
        if ds == 0:
            src, dst = base.at[4 if db == 1 else 1], base.at[0 if db == 1 else 5]
        else:
            side = 0 if ds == 1 else 1
            if db == 0:
                src, dst = face.at[side], zin.at[side, pl.ds(1, 4)]
            else:
                src, dst = face.at[side, 3 if db == 1 else 0], zin.at[side, 0 if db == 1 else 5]
        copies.append(send(src, dst, s.at[n], r.at[n], neighbour(ds, db)))
    order = (2, 3, 4, 5, 6, 7, 0, 1)
    for n in order:
        copies[n].start()
    return copies


def shifted_copies(base, zin, ext):
    def step(i, carry):
        v = base[i]
        wide = v.astype(F32)
        row = lax.broadcasted_iota(jnp.int32, wide.shape, 1)
        before = jnp.broadcast_to(zin[0, i].astype(F32)[:, None, :], wide.shape)
        after = jnp.broadcast_to(zin[1, i].astype(F32)[:, None, :], wide.shape)
        low = jnp.where(row == 15, after, pltpu.roll(wide, 15, 1)).astype(BF16)
        high = jnp.where(row == 0, before, pltpu.roll(wide, 1, 1)).astype(BF16)
        for c, w in enumerate((low, v, high)):
            ext[c, i, pl.ds(1, 8)] = w
            ext[c, i, 0] = w[7]
            ext[c, i, 9] = w[0]
        return carry

    lax.fori_loop(0, 6, step, 0)


def triple(ext, a, b, order):
    parts = [ext[1 + c, pl.ds(1 - a, 4), pl.ds(1 - b, 8)].reshape(512, 128) for c in order]
    return jnp.concatenate(parts, axis=1)


def transpose_conv(ext, w):
    total = None
    for a in (-1, 0, 1):
        for b in (-1, 0, 1):
            k = 9 * (a + 1) + 3 * (b + 1)
            right = jnp.concatenate([w[k], w[k + 1], w[k + 2]], axis=1)
            term = lax.dot_general(triple(ext, a, b, (-1, 0, 1)), right, (((1,), (1,)), ((), ())), preferred_element_type=F32)
            total = term if total is None else total + term
    return total


def put(part, g, k, value):
    value = value.astype(BF16)
    for j in range(8):
        lo, hi = max(128 * k, ROWS * j), min(128 * k + 128, ROWS * j + ROWS)
        if lo < hi:
            part[g, j % 2, j // 2, lo - ROWS * j : hi - ROWS * j] = value[lo - 128 * k : hi - 128 * k]


def body(scale, inputs_hbm, pre_hbm, occ_hbm, grad_out_hbm, w1_hbm, w2_hbm, grad_in, first_hbm, second_hbm, pre, occ_in, grad_out, act, slope, w1, w2, bases, faces, zins, ext, part, pair, summed, stage, mid, first_in, second_out, second_in, tiles, deep_in, final, out, load_sem, halo_s, halo_r, store_sem, sems):
    x, y, z, core = coordinates()
    pair_s, pair_r, first_s, first_r, second_s, second_r, deep_s, deep_r, back_s, back_r = sems[:10]
    up2_s, up2_r, up1_s, up1_r, last_s, last_r = sems[10:]
    partner = device(x, y, z, 1 - core)
    own = (x, y)

    def peer(axis, d):
        if axis == 0:
            return device((x + d) % SIDE, y, z, core)
        return device(x, (y + d) % SIDE, z, core)

    def deep(d):
        return device(x, y, (z + d) % DEPTH, core)

    barrier = pltpu.get_barrier_semaphore()
    everyone = [neighbour(ds, db) for ds, db in reversed(NEAR)] + [deep(d) for d in range(1, DEPTH)]
    everyone += [peer(h, d) for h in (0, 1) for d in (1, 2, 3)] + [partner]
    for to in everyone:
        pl.semaphore_signal(barrier, inc=1, device_id=to, device_id_type=pl.DeviceIdType.MESH)
    loads = [
        pltpu.make_async_copy(src, dst, load_sem.at[n])
        for n, (src, dst) in enumerate(
            (
                (occ_hbm, occ_in),
                (grad_out_hbm, grad_out),
                (inputs_hbm, bases.at[1, pl.ds(1, 4)]),
                (pre_hbm, pre),
                (w2_hbm, w2),
                (w1_hbm, w1),
            )
        )
    ]
    for load in loads:
        load.start()
    for g in (0, 1):
        for c in (0, 1):
            for i in range(SIDE):
                part[g, c, i, ROWS:] = jnp.zeros((PADDED - ROWS, 128), BF16)

    def mask(i):
        row = occ_in[i].astype(F32)
        wide = jnp.broadcast_to(row[:, None, :], (8, 16, 16))
        here = lax.broadcasted_iota(jnp.int32, wide.shape, 1) == lax.broadcasted_iota(jnp.int32, wide.shape, 2)
        return jnp.sum(jnp.where(here, wide, 0.0), axis=2, keepdims=True)

    def set_faces(f, i, value):
        faces[f, 0, i] = value[:, 15, :].astype(BF16)
        faces[f, 1, i] = value[:, 0, :].astype(BF16)

    def masked(i, carry):
        value = grad_out[i].astype(F32) * mask(i)
        bases[0, i + 1] = value.astype(BF16)
        set_faces(0, i, value)
        set_faces(1, i, bases[1, i + 1].astype(F32))
        return carry

    for n in (0, 1, 2):
        loads[n].wait()
    lax.fori_loop(0, 4, masked, 0)
    pl.semaphore_wait(barrier, len(everyone))

    def start_halo(f):
        return exchange(bases.at[f], faces.at[f], zins.at[f], halo_s.at[f], halo_r.at[f])

    halos = [start_halo(0)]

    def pointwise(i, carry):
        v, occ = pre[i].astype(F32), mask(i)
        sig = 1.0 / (1.0 + jnp.exp(-v))
        act[i] = (v * sig * occ).astype(BF16)
        slope[i] = occ * sig * (1.0 + v * (1.0 - sig))
        return carry

    loads[3].wait()
    lax.fori_loop(0, 4, pointwise, 0)
    halos.append(start_halo(1))
    act_t = act[...].reshape(512, 128).T
    loads[4].wait()
    loads[5].wait()
    for copy in halos[0]:
        copy.wait_recv()
    shifted_copies(bases.at[0], zins.at[0], ext.at[0])

    pairs, firsts, seconds = {}, {}, {}

    def pair_copy(h, i):
        return send(part.at[h, 1 - core, i], pair.at[h, i], pair_s.at[h, i], pair_r.at[h, i], partner)

    def start_pairs(h, ab):
        for i in range(SIDE):
            if 384 * ab < 2 * ROWS * (i + 1) <= 384 * (ab + 1):
                pairs[h, i] = pair_copy(h, i)
                pairs[h, i].start()

    def start_firsts(h):
        def add(d):
            slot = (own[h] + d) % SIDE
            pair_copy(h, slot).wait_recv()
            total = part[h, core, slot].astype(F32) + pair[h, slot].astype(F32)
            summed[h, slot] = total.astype(BF16)
            return summed.at[h, slot]

        def go(n, src, dst, d):
            firsts[h, n] = send(src, dst, first_s.at[h, n], first_r.at[h, n], peer(h, d))
            firsts[h, n].start()

        low, high = pl.ds(0, HALF), pl.ds(HALF, HALF)
        ref = add(2)
        go(0, ref.at[low], stage.at[h, 0], 1)
        go(1, ref.at[high], stage.at[h, 1], 3)
        go(2, add(1).at[high], first_in.at[h, 0, high], 1)
        go(3, add(3).at[low], first_in.at[h, 1, low], 3)
        add(0)

    def forward_firsts(h):
        for n, d in ((0, 1), (1, 3)):
            slot = (own[h] + d) % SIDE
            rows = pl.ds(HALF * n, HALF)
            firsts[h, n].wait_recv()
            mid[h, n] = (summed[h, slot, rows].astype(F32) + stage[h, n].astype(F32)).astype(BF16)
            firsts[h, 4 + n] = send(mid.at[h, n], first_in.at[h, n, rows], first_s.at[h, 4 + n], first_r.at[h, 4 + n], peer(h, d))
            firsts[h, 4 + n].start()

    def start_seconds(h):
        for n in (2, 3, 4, 5):
            firsts[h, n].wait_recv()
        total = summed[h, own[h]].astype(F32) + first_in[h, 0].astype(F32) + first_in[h, 1].astype(F32)
        second_out[h] = total.astype(BF16).reshape(SIDE, PIECE, 128)
        for d in (2, 1, 3):
            slot = (own[1 - h] + d) % SIDE
            seconds[h, d] = send(second_out.at[h, slot], second_in.at[h, d - 1], second_s.at[h, d - 1], second_r.at[h, d - 1], peer(1 - h, d))
            seconds[h, d].start()

    for a in (-1, 0, 1):
        for b in (-1, 0, 1):
            k = 9 * (a + 1) + 3 * (b + 1)
            term = jnp.dot(act_t, triple(ext.at[0], a, b, (-1, 0, 1)), preferred_element_type=F32)
            for c in range(3):
                put(part, 0, k + c, term[:, 128 * c : 128 * c + 128])
            start_pairs(0, k // 3)
    grad_act = transpose_conv(ext.at[0], w2)
    grad_pre = (grad_act.reshape(4, 8, 16, 128) * slope[...]).astype(BF16)
    bases[2, pl.ds(1, 4)] = grad_pre
    wide = grad_pre.astype(F32)
    faces[2, 0] = wide[:, :, 15, :].astype(BF16)
    faces[2, 1] = wide[:, :, 0, :].astype(BF16)
    halos.append(start_halo(2))
    start_firsts(0)
    for copy in halos[1]:
        copy.wait_recv()
    shifted_copies(bases.at[1], zins.at[1], ext.at[1])
    forward_firsts(0)
    grad_t = grad_pre.reshape(512, 128).T
    for a in (-1, 0, 1):
        for b in (-1, 0, 1):
            k = 9 * (a + 1) + 3 * (b + 1)
            term = jnp.dot(grad_t, triple(ext.at[1], -a, -b, (1, 0, -1)), preferred_element_type=F32)
            for c in range(3):
                put(part, 1, k + c, term[:, 128 * c : 128 * c + 128].T)
            start_pairs(1, k // 3)
    far = sorted(range(1, DEPTH), key=lambda d: -min(d, DEPTH - d))
    owned = (range(0, 7), range(7, 14))

    def deep_copy(t):
        slot = (t - z + DEPTH) % DEPTH - 1
        return send(tiles.at[t], deep_in.at[slot], deep_s.at[t], deep_r.at[slot], device(x, y, t, core))

    def back_copy(d):
        return send(final.at[z], final.at[z], back_s.at[d], back_r.at[z], deep(d))

    def start_deeps(h):
        for d in (1, 2, 3):
            seconds[h, d].wait_recv()
        total = second_out[h, own[1 - h]].astype(F32)
        for d in (1, 2, 3):
            total = total + second_in[h, d - 1].astype(F32)
        tiles[7 * h : 7 * h + 7] = total.astype(BF16).reshape(7, TILE, 128)
        for t in owned[h]:

            @pl.when(z != t)
            def _():
                deep_copy(t).start()

    def start_backs(h):
        @pl.when(z // 7 == h)
        def _():
            total = tiles[z].astype(F32)
            for d in reversed(far):
                send(tiles.at[z], deep_in.at[d - 1], deep_s.at[0], deep_r.at[d - 1], deep(d)).wait_recv()
                total = total + deep_in[d - 1].astype(F32)
            final[z] = (total * scale).astype(BF16)
            for d in far:
                back_copy(d).start()

    def wait_backs(h):
        for t in owned[h]:

            @pl.when(z != t)
            def _():
                send(final.at[t], final.at[t], back_s.at[0], back_r.at[t], deep(1)).wait_recv()

    start_firsts(1)
    start_seconds(0)
    forward_firsts(1)
    start_deeps(0)
    start_seconds(1)
    start_deeps(1)
    start_backs(0)

    for copy in halos[2]:
        copy.wait_recv()
    shifted_copies(bases.at[2], zins.at[2], ext.at[0])
    back = transpose_conv(ext.at[0], w1)
    grad_in[...] = (grad_out[...].astype(F32) + back.reshape(4, 8, 16, 128)).astype(BF16)

    start_backs(1)
    up2 = {}
    for h in (0, 1):
        wait_backs(h)
        rows = pl.ds(pl.multiple_of(own[1 - h] * PIECE, PIECE), PIECE)
        out[h, core, own[h], rows] = final[7 * h : 7 * h + 7].reshape(PIECE, 128)
        place = out.at[h, core, own[h], rows]
        for d in (2, 1, 3):
            up2[h, d] = send(place, place, up2_s.at[h, d - 1], up2_r.at[h, d - 1], peer(1 - h, d))
            up2[h, d].start()
    up1, lasts, stores = {}, {}, []

    halves = (pl.ds(0, HALF), pl.ds(HALF, HALF))
    lengths = (HALF, ROWS - HALF)

    def store(h, c, slot, n):
        rows = pl.ds(pl.multiple_of((2 * slot + c) * ROWS + HALF * n, TILE), lengths[n])
        result = (second_hbm, first_hbm)[h]
        src = out.at[h, c, slot, pl.ds(HALF * n, lengths[n])]
        stores.append(pltpu.make_async_copy(src, result.at[rows], store_sem.at[h, c, slot, n]))
        stores[-1].start()

    def up(h, m, came, n, d):
        place = out.at[h, core, (own[h] + came) % SIDE, halves[n]]
        up1[h, m] = send(place, place, up1_s.at[h, m], up1_r.at[h, m], peer(h, d))
        up1[h, m].start()

    def share(h, came, n):
        slot = (own[h] + came) % SIDE
        place = out.at[h, core, slot, halves[n]]
        lasts[h, came, n] = send(place, place, last_s.at[h, came, n], last_r.at[h, came, n], partner)
        lasts[h, came, n].start()
        store(h, core, slot, n)

    def keep(h, came, n):
        lasts[h, came, n].wait_recv()
        store(h, 1 - core, (own[h] + came) % SIDE, n)

    def own_chunk(h):
        for d in (1, 2, 3):
            up2[h, d].wait_recv()
        up(h, 0, 0, 0, 1)
        up(h, 1, 0, 1, 3)
        up(h, 2, 0, 1, 1)
        up(h, 3, 0, 0, 3)
        share(h, 0, 0)
        share(h, 0, 1)

    def forward(h):
        up1[h, 0].wait_recv()
        up(h, 4, 3, 0, 1)
        up1[h, 1].wait_recv()
        up(h, 5, 1, 1, 3)
        share(h, 3, 0)
        share(h, 1, 1)

    def others(h):
        up1[h, 2].wait_recv()
        share(h, 3, 1)
        up1[h, 3].wait_recv()
        share(h, 1, 0)
        for n in (0, 1):
            keep(h, 0, n)
        keep(h, 3, 0)
        keep(h, 1, 1)

    def opposite(h):
        up1[h, 4].wait_recv()
        share(h, 2, 0)
        up1[h, 5].wait_recv()
        share(h, 2, 1)

    def rest(h):
        keep(h, 3, 1)
        keep(h, 1, 0)
        for n in (0, 1):
            keep(h, 2, n)

    own_chunk(0)
    forward(0)
    own_chunk(1)
    others(0)
    forward(1)
    opposite(0)
    others(1)
    opposite(1)
    rest(0)
    rest(1)
    for t in range(14):

        @pl.when(z != t)
        def _():
            deep_copy(t).wait_send()

    @pl.when(z < 14)
    def _():
        for d in range(1, DEPTH):
            back_copy(d).wait_send()

    for group in (pairs, firsts, seconds, up2, up1, lasts):
        for copy in group.values():
            copy.wait_send()
    for copies in halos:
        for copy in copies:
            copy.wait_send()
    for copy in stores:
        copy.wait()


def settle(sources, results, slots, sems):
    for n, (src, slot) in enumerate(zip(sources, slots)):
        pltpu.make_async_copy(src, slot, sems.at[0, n]).start()
    for n, (src, slot, dst) in enumerate(zip(sources, slots, results)):
        pltpu.make_async_copy(src, slot, sems.at[0, n]).wait()
        pltpu.make_async_copy(slot, dst, sems.at[1, n]).start()
    for n, (slot, dst) in enumerate(zip(slots, results)):
        pltpu.make_async_copy(slot, dst, sems.at[1, n]).wait()


def settled(*arrays):
    def kernel(*refs):
        count = len(arrays)
        sources, results, slots, sems = refs[:count], refs[count : 2 * count], refs[2 * count : 3 * count], refs[-1]
        cuts = [(n, pl.ds(i, a.shape[0] // parts)) for n, (a, parts) in enumerate(zip(arrays, (1, 3, 3)))
                for i in range(0, a.shape[0], a.shape[0] // parts)]
        settle(*([refs_[n].at[cut] for n, cut in cuts] for refs_ in (sources, results, slots)), sems)

    hbm = pl.BlockSpec(memory_space=pl.ANY)
    return pl.pallas_call(
        kernel,
        out_shape=tuple(jax.ShapeDtypeStruct(a.shape, a.dtype) for a in arrays),
        in_specs=[hbm] * len(arrays),
        out_specs=(hbm,) * len(arrays),
        scratch_shapes=[pltpu.VMEM(a.shape, a.dtype) for a in arrays] + [pltpu.SemaphoreType.DMA((2, 7))],
        name="settle",
    )(*arrays)


def per_device(inputs, pre_first, occupancy, grad_out, w_first, w_second):
    size_x, size_y, size_z, chans = inputs.shape
    cells_all = size_x * lax.axis_size("brick") * size_y * size_z * lax.axis_size("slab")
    scale = 10.0 / cells_all**0.5
    dma = pltpu.SemaphoreType.DMA
    shapes = [(2, 4), (2, 4), (2, 6), (2, 6), (2, 3), (2, 3), (16,), (16,), (16,), (16,), (2, 3), (2, 3), (2, 6), (2, 6), (2, 4, 2), (2, 4, 2)]

    def kernel(*refs):
        body(scale, *refs[:36], refs[36:])

    vmem = pl.BlockSpec(memory_space=pltpu.VMEM)
    hbm = pl.BlockSpec(memory_space=pl.ANY)
    grad_in, grad_first, grad_second = pl.pallas_call(
        kernel,
        out_shape=(
            jax.ShapeDtypeStruct(inputs.shape, BF16),
            jax.ShapeDtypeStruct((8 * ROWS, 128), BF16),
            jax.ShapeDtypeStruct((8 * ROWS, 128), BF16),
        ),
        in_specs=[hbm] * 6,
        out_specs=(vmem, hbm, hbm),
        scratch_shapes=[
            pltpu.VMEM((4, 8, 16, 128), BF16),
            pltpu.VMEM((4, 8, 16), jnp.int32),
            pltpu.VMEM((4, 8, 16, 128), BF16),
            pltpu.VMEM((4, 8, 16, 128), BF16),
            pltpu.VMEM((4, 8, 16, 128), F32),
            pltpu.VMEM((27, 128, 128), BF16),
            pltpu.VMEM((27, 128, 128), BF16),
            pltpu.VMEM((3, 6, 8, 16, 128), BF16),
            pltpu.VMEM((3, 2, 4, 8, 128), BF16),
            pltpu.VMEM((3, 2, 6, 8, 128), BF16),
            pltpu.VMEM((2, 3, 6, 10, 16, 128), BF16),
            pltpu.VMEM((2, 2, SIDE, PADDED, 128), BF16),
            pltpu.VMEM((2, SIDE, PADDED, 128), BF16),
            pltpu.VMEM((2, SIDE, PADDED, 128), BF16),
            pltpu.VMEM((2, 2, HALF, 128), BF16),
            pltpu.VMEM((2, 2, HALF, 128), BF16),
            pltpu.VMEM((2, 2, PADDED, 128), BF16),
            pltpu.VMEM((2, SIDE, PIECE, 128), BF16),
            pltpu.VMEM((2, 3, PIECE, 128), BF16),
            pltpu.VMEM((DEPTH, TILE, 128), BF16),
            pltpu.VMEM((DEPTH - 1, TILE, 128), BF16),
            pltpu.VMEM((DEPTH, TILE, 128), BF16),
            pltpu.VMEM((2, 2, SIDE, PADDED, 128), BF16),
            dma((6,)), dma((3, 8)), dma((3, 8)), dma((2, 2, SIDE, 2)),
        ] + [dma(s) for s in shapes],
        compiler_params=pltpu.CompilerParams(collective_id=0, has_side_effects=True),
        name="block_backward",
    )(inputs, pre_first, occupancy, grad_out, w_first, w_second)
    return settled(grad_in, grad_first.reshape(w_first.shape), grad_second.reshape(w_second.shape))


def solution(mesh):
    in_specs = (
        P("brick", None, "slab", None),
        P("brick", None, "slab", None),
        P("brick", None, "slab"),
        P("brick", None, "slab", None),
        P(),
        P(),
    )
    out_specs = (P("brick", None, "slab", None), P(), P())
    return jax.shard_map(
        per_device, mesh=mesh, in_specs=in_specs, out_specs=out_specs, check_vma=False
    )
```
